32 devices in a mesh: seq: 8 (over y, x, core), ch: 4 (over z).
Axes of the slice: x: 2, y: 2, z: 4, core: 2. Of those that a mesh axis runs over, the one named last changes fastest.
Arguments:
- token_ids: int32 [2048], P('seq'), may hold values from 65 to 84, as said below
- embedding: bfloat16 [512, 8192], P(None, 'ch'), may hold values from -1200 to 1200
- norm_gain: float32 [8192], P('ch'), may hold values from 0.5 to 1.5
- conv_weight: float32 [3, 7, 8192], P(None, None, 'ch'), may hold values from -2 to 2
- pole_rates: float32 [16, 8192], P(None, 'ch'), may hold values from 0.001 to 0.105
- residues: float32 [16, 8192], P(None, 'ch'), may hold values from -70 to 70
- skip_gain: float32 [8192], P('ch'), may hold values from -1.5 to 1.5
- cotangent: bfloat16 [2048, 8192], P('seq', 'ch'), may hold values from -6 to 6
Outputs:
- hyena_out: bfloat16 [2048, 8192], P('seq', 'ch')
- grad_normed: bfloat16 [2048, 8192], P('seq', 'ch')
- grad_conv: float32 [3, 7, 8192], P(None, None, 'ch')
- grad_residues: float32 [16, 8192], P(None, 'ch')
- grad_skip: float32 [8192], P('ch')
The draws below stay inside these ranges and needn't reach their ends.
Inputs may be any that keep to these rules, and one draw needn't show every extreme that they name: `token_ids`: every token is the byte code of A, C, G or T.
All inputs are finite; a program needn't handle non-finite values.
Results may differ from the reference program's by a relative error of at most 0.03.
Values may be sent and summed in bfloat16 or wider, within the bound.
A program may use at most 128 MiB of HBM per device.

```python
import jax
import jax.numpy as jnp
from jax import lax

D = 8192
VOCAB = 512
POLES = 16
TAPS = 7
TOKENS = 2048


def draw_token_ids(key, part):
    picks = jax.random.randint(jax.random.fold_in(key, 11), (TOKENS,), 0, 4)
    return (65 + 2 * (picks >= 1) + 4 * (picks >= 2) + 13 * (picks >= 3)).astype(jnp.int32)


def draw_embedding(key, part):
    base_key = jax.random.fold_in(key, 23)
    key_base, key_rows, key_cols = jax.random.split(base_key, 3)
    position = jnp.arange(D, dtype=jnp.float32) / max(D - 1, 1)
    row_scale = jnp.power(10.0, jax.random.uniform(key_rows, (VOCAB, 1), jnp.float32))
    col_base = jnp.power(10.0, jax.random.uniform(key_cols, (1, D), jnp.float32))
    values = jax.random.truncated_normal(key_base, -4.0, 4.0, (VOCAB, D), jnp.float32)
    col_scale = col_base * jnp.power(3.0, position)[None, :]
    return (values * row_scale * col_scale).astype(jnp.bfloat16)


def cluster_draw(key):
    base_key = jax.random.fold_in(key, 41)
    key_base, key_growth, key_magnitude, key_polarity = jax.random.split(base_key, 4)
    clusters = POLES // 4
    grid_shape = (clusters, D)
    growth = jax.random.uniform(key_growth, grid_shape, jnp.float32, 1.35, 1.6)
    fastest = 0.1049 / (growth * growth * growth)
    spread = jnp.log(fastest / 0.001)
    slowest = 0.001 * jnp.exp(spread * jax.random.uniform(key_base, grid_shape, jnp.float32))
    raised = [jnp.ones_like(growth), growth, growth * growth, growth * growth * growth]
    decay_rates = jnp.stack([slowest * factor for factor in raised], 1).reshape(POLES, D)
    magnitude = jnp.exp(jax.random.uniform(key_magnitude, grid_shape, jnp.float32, -0.693, 0.693))
    polarity = jnp.where(jax.random.uniform(key_polarity, grid_shape, jnp.float32) < 0.5, -1.0, 1.0)
    amplitude = 10.0 * magnitude * polarity * slowest / jnp.sqrt(0.035)
    weights = []
    for member in range(4):
        denominator = jnp.ones_like(growth)
        for partner in range(4):
            if partner != member:
                denominator = denominator * (raised[partner] - raised[member])
        weights.append(-amplitude * raised[member] / denominator)
    residue_table = jnp.stack(weights, 1).reshape(POLES, D)
    return (decay_rates, residue_table)


def draw_pole_rates(key, part):
    return cluster_draw(key)[0].astype(jnp.float32)


def draw_residues(key, part):
    return cluster_draw(key)[1].astype(jnp.float32)


def block_scale(stream_key, extent, cuts, least, top_value):
    level, own = 1.0, jax.random.fold_in(stream_key, 6)
    for dim, shards_of in cuts:
        heights = jnp.exp(jax.random.uniform(jax.random.fold_in(own, dim), (shards_of,), jnp.float32, least / len(cuts), top_value / len(cuts)))
        level = level * jnp.repeat(heights, extent[dim] // shards_of).reshape([-1 if axis == dim else 1 for axis in range(len(extent))])
    return level


def gaussian(key, extent, width, most, cuts=(), held_as=jnp.bfloat16):
    entries = jax.random.normal(key, extent, jnp.float32) * width
    if len(cuts) > 0:
        entries = block_scale(key, extent, cuts, -0.22, 0.18) * entries
    return jnp.clip(entries, min=-most, max=most).astype(held_as)


def setup_inputs(seed: int = 0) -> dict:
    key_of = jax.random.split(jax.random.key(seed), 9)
    token_ids = draw_token_ids(jax.random.fold_in(key_of[8], 71), 0)
    embedding = draw_embedding(jax.random.fold_in(key_of[8], 71), 0)
    norm_gain = jnp.clip(1.0 + 0.1 * jax.random.normal(key_of[2], (D,), jnp.float32), 0.5, 1.5)
    conv_weight = gaussian(key_of[3], (3, TAPS, D), TAPS ** -0.5, 2.0, ((2, 4),), jnp.float32)
    pole_rates = draw_pole_rates(jax.random.fold_in(key_of[8], 71), 0)
    residues = draw_residues(jax.random.fold_in(key_of[8], 71), 0)
    skip_gain = gaussian(key_of[6], (D,), 0.25, 1.5, ((0, 4),), jnp.float32)
    cotangent = gaussian(key_of[7], (TOKENS, D), 1.0, 6.0, ((0, 8), (1, 4)))
    return {"token_ids": token_ids, "embedding": embedding, "norm_gain": norm_gain, "conv_weight": conv_weight, "pole_rates": pole_rates, "residues": residues, "skip_gain": skip_gain, "cotangent": cotangent}


def block_pass(scale_rows, embed_block, upstream, gain_block, weight_block, rate_block, residue_block, skip_block):
    length = embed_block.shape[0]
    block_width = embed_block.shape[1]
    normed = (embed_block.astype(jnp.float32) * scale_rows[:, None] * gain_block[None, :]).astype(jnp.bfloat16)
    normed = lax.optimization_barrier(normed)
    padded = jnp.concatenate([jnp.zeros((TAPS - 1, block_width), jnp.bfloat16), normed], 0).astype(jnp.float32)
    features = []
    for feature in range(3):
        summed = jnp.zeros((length, block_width), jnp.float32)
        for offset in range(TAPS):
            summed = summed + weight_block[feature, offset][None, :] * padded[TAPS - 1 - offset:TAPS - 1 - offset + length]
        features.append(summed)
    features = lax.optimization_barrier(jnp.stack(features).astype(jnp.bfloat16)).astype(jnp.float32)
    query_feat = features[0]
    key_feat = features[1]
    value_feat = features[2]
    mixed_kv = key_feat * value_feat
    grad_long = upstream.astype(jnp.float32) * query_feat
    decay_step = jnp.exp(-rate_block)
    zeros_state = jnp.zeros(rate_block.shape, jnp.float32)

    def forward_step(carried, inputs):
        state_now, residue_acc = carried
        mixed_row, grad_row = inputs
        state_now = decay_step * state_now + mixed_row[None, :]
        long_row = lax.optimization_barrier(jnp.sum(residue_block * state_now, 0)) + skip_block * mixed_row
        return ((state_now, residue_acc + grad_row[None, :] * state_now), long_row)
    (spent_state, grad_res), long_conv = lax.scan(forward_step, (zeros_state, zeros_state), (mixed_kv, grad_long))

    def backward_step(adjoint, grad_row):
        adjoint = decay_step * adjoint + grad_row[None, :]
        return (adjoint, skip_block * grad_row + lax.optimization_barrier(jnp.sum(residue_block * adjoint, 0)))
    spent_adjoint, grad_mixed = lax.scan(backward_step, zeros_state, grad_long, reverse=True)
    hyena_out = (query_feat * long_conv).astype(jnp.bfloat16)
    grad_skip = lax.optimization_barrier(jnp.sum(grad_long * mixed_kv, 0))
    feature_grads = jnp.stack([upstream.astype(jnp.float32) * long_conv, grad_mixed * value_feat, grad_mixed * key_feat]).astype(jnp.bfloat16)
    grads_f32 = lax.optimization_barrier(feature_grads).astype(jnp.float32)
    grad_conv = jnp.stack([jnp.stack([lax.optimization_barrier(jnp.sum(grads_f32[feature] * padded[TAPS - 1 - offset:TAPS - 1 - offset + length], 0)) for offset in range(TAPS)]) for feature in range(3)])
    trailing = jnp.concatenate([grads_f32, jnp.zeros((3, TAPS - 1, block_width), jnp.float32)], 1)
    grad_input = jnp.zeros((length, block_width), jnp.float32)
    for feature in range(3):
        for offset in range(TAPS):
            grad_input = grad_input + weight_block[feature, offset][None, :] * trailing[feature, offset:offset + length]
    return (hyena_out, grad_input.astype(jnp.bfloat16), grad_conv, grad_res, grad_skip)

def reference(token_ids, embedding, norm_gain, conv_weight, pole_rates, residues, skip_gain, cotangent):
    embedded = embedding[token_ids]
    widened = embedded.astype(jnp.float32)
    scale_rows = lax.rsqrt(lax.optimization_barrier(jnp.mean(widened * widened, axis=1)) + 1e-05)
    block_width = min(D, 1024)
    blocks = D // block_width

    def to_blocks(array):
        return jnp.moveaxis(array.reshape(array.shape[:-1] + (blocks, block_width)), -2, 0)

    def from_blocks(array):
        return jnp.moveaxis(array, 0, -2).reshape(array.shape[1:-1] + (D,))

    def one_block(pieces):
        return block_pass(scale_rows, pieces[0], pieces[1], pieces[2], pieces[3], pieces[4], pieces[5], pieces[6])
    results = lax.map(one_block, (to_blocks(embedded), to_blocks(cotangent), to_blocks(norm_gain), to_blocks(conv_weight), to_blocks(pole_rates), to_blocks(residues), to_blocks(skip_gain)))
    return (from_blocks(results[0]), from_blocks(results[1]), from_blocks(results[2]), from_blocks(results[3]), from_blocks(results[4]))
```

```python
import functools

import jax
import jax.numpy as jnp
from jax import lax
from jax.experimental import pallas as pl
from jax.experimental.pallas import tpu as pltpu
from jax.sharding import PartitionSpec as P

TAPS = 7
CODES = (65, 67, 71, 84)
MESH = pl.DeviceIdType.MESH
F32 = jnp.float32
BF16 = jnp.bfloat16
LANES = 128
SUB = 8
UNROLL = 8
BAND = 32
VLIMIT = 60 * 1024 * 1024


def greet(peers):
    barrier = pltpu.get_barrier_semaphore()
    for peer in peers:
        pl.semaphore_signal(barrier, inc=1, device_id=peer, device_id_type=MESH)


def greeted(peers):
    pl.semaphore_wait(pltpu.get_barrier_semaphore(), len(peers))


def remote(src, dst, send_sem, recv_sem, peer):
    return pltpu.make_async_remote_copy(
        src_ref=src, dst_ref=dst, send_sem=send_sem, recv_sem=recv_sem,
        device_id=peer, device_id_type=MESH,
    )


def mega_kernel(
    n_seq, n_ch, poles,
    ids_in, emb_ref, gain_in, w_in, rate_in, res_in, skip_in, ct_in,
    hyena_ref, gn_ref, conv_ref, gr_out_ref, gskip_out_ref,
    ids_ref, gain_ref, w_ref, rate_ref, res_ref, skip_in_ref, ct_ref, load_sem,
    part, ss_got, prev_got, feat_ref, y_ref, gm_ref, ot_ref, n4_ref, ends_ref, in_ref, gr_ref, gskip_ref,
    p_ref, r_ref, decay_ref, skip_ref, xs, gs, table, got, out, fg_ref, head_ref, tail,
    terms, terms_ref, tgot, total, sums_ref, wide, pad,
    emb_rows, emb_sem, ss_send, ss_recv, halo_sem, f_send, f_recv, fb_send, fb_recv, a_send, a_recv, ab_send, ab_recv,
    t_send, t_recv, tb_send, tb_recv,
):
    me = lax.axis_index("seq")
    ch = lax.axis_index("ch")
    length, chans = ct_ref.shape
    width = chans * n_ch
    nb = chans // LANES
    lines = poles * nb
    first = lines + nb
    rows_used = first + 3 * TAPS * nb
    peer = [lax.rem(me + o, n_seq) for o in range(n_seq)]
    ch_peer = [lax.rem(ch + o, n_ch) for o in range(n_ch)]

    peers = [{"seq": peer[o]} for o in range(1, n_seq)] + [{"ch": ch_peer[o]} for o in range(1, n_ch)]
    greet(peers)
    low_row = min(CODES) // BAND * BAND
    fetch = pltpu.make_async_copy(emb_ref.at[low_row : low_row + BAND, :], emb_rows, emb_sem)
    fetch.start()
    loads = [
        pltpu.make_async_copy(src, dst, load_sem.at[i])
        for i, (src, dst) in enumerate((
            (rate_in, rate_ref), (res_in, res_ref), (skip_in, skip_in_ref), (ids_in, ids_ref), (gain_in, gain_ref),
            (w_in, w_ref), (ct_in, ct_ref),
        ))
    ]
    for load in loads:
        load.start()
    for load in loads[:3]:
        load.wait()
    for k in range(nb):
        lanes = slice(k * LANES, (k + 1) * LANES)
        rates = rate_ref[:, lanes]
        rows = pl.ds(k, poles, stride=nb)
        p_ref[rows, :] = jnp.exp(-rates)
        decay_ref[rows, :] = jnp.exp(-rates * length)
        r_ref[rows, :] = res_ref[:, lanes]
        skip_ref[k : k + 1, :] = skip_in_ref[:, lanes]
    fetch.wait()
    emb = jnp.concatenate(
        [emb_rows[v - low_row : v - low_row + 1, :].astype(F32) for v in CODES]
        + [jnp.zeros((SUB - len(CODES), chans), F32)],
        0,
    )
    squares = jnp.broadcast_to(jnp.sum(emb * emb, axis=1, keepdims=True), (SUB, LANES))
    part[...] = squares
    greeted(peers)
    ids_copy = remote(ids_in, prev_got, halo_sem.at[0], halo_sem.at[1], {"seq": peer[1]})
    ids_copy.start()
    copies = []
    for o in range(1, n_ch):
        copy = remote(part, ss_got.at[o], ss_send.at[o], ss_recv.at[o], {"ch": ch_peer[o]})
        copy.start()
        copies.append(copy)
    for load in loads[3:6]:
        load.wait()
    for o in range(1, n_ch):
        copies[o - 1].wait()
        squares = squares + ss_got[o]
    ids_copy.wait()
    prev = jnp.where(me > 0, prev_got[...], -1)
    scale = lax.rsqrt(squares / width + 1e-05)[:, :1]
    n4 = (emb * scale * gain_ref[...]).astype(BF16).astype(F32)
    n4_ref[...] = n4
    zero_rows = jnp.zeros((SUB, chans), F32)
    for f in range(3):
        full = jnp.concatenate(
            [w_ref[f, i : i + 1, :] * n4 for i in range(TAPS)] + [zero_rows], 0
        )
        high = full.astype(BF16)
        rest = full - high.astype(F32)
        mid = rest.astype(BF16)
        low = (rest - mid.astype(F32)).astype(BF16)
        table[f, 0 : 8 * SUB, :] = high
        table[f, 8 * SUB : 16 * SUB, :] = mid
        table[f, 16 * SUB : 24 * SUB, :] = low
    row = lax.broadcasted_iota(jnp.int32, (SUB, length), 0)
    code = jnp.full((SUB, length), -2, jnp.int32)
    for a, value in enumerate(CODES):
        code = jnp.where(row == a, value, code)
    ext = jnp.concatenate([prev, ids_ref[...]], 1)
    hits = [
        jnp.where(ext[:, length - i : 2 * length - i] == code, 1.0, 0.0).astype(F32) for i in range(TAPS)
    ] + [jnp.zeros((SUB, length), F32)]
    onehot = jnp.concatenate(hits, 0)
    ot_ref[...] = onehot.astype(BF16)
    picks = jnp.transpose(jnp.concatenate([onehot] * 3, 0)).astype(BF16)

    def features(kb, carry):
        lanes = pl.ds(pl.multiple_of(kb * 256, 256), 256)
        parts = []
        for f in range(3):
            val = jnp.dot(picks, table[f, :, lanes], preferred_element_type=F32).astype(BF16)
            feat_ref[f, :, lanes] = val
            parts.append(val.astype(F32))
        x = parts[1] * parts[2]
        g = ct_ref[:, lanes].astype(F32) * parts[0]
        for s in range(2):
            xs[pl.ds(kb * 2 + s, length, stride=nb), :] = x[:, s * LANES : (s + 1) * LANES]
            gs[pl.ds(kb * 2 + s, length, stride=nb), :] = g[:, s * LANES : (s + 1) * LANES]
        return carry

    loads[6].wait()
    lax.fori_loop(0, chans // 256, features, 0)


    rp = lines // n_seq
    chunk = lambda k: pl.ds(pl.multiple_of(k * rp, rp), rp)

    def send_ends(side, send, recv):
        started = []
        for o in range(1, n_seq):
            copy = remote(
                ends_ref.at[side, chunk(peer[o]), :], got.at[side, me], send.at[o], recv.at[o], {"seq": peer[o]}
            )
            copy.start()
            started.append(copy)
        got[side, me] = ends_ref[side, chunk(me), :]
        return started

    def send_carries(side, started, send, recv):
        for copy in started:
            copy.wait()
        decay = decay_ref[chunk(me), :]
        state = jnp.zeros_like(decay)
        for e in reversed(range(n_seq)) if side else range(n_seq):
            out[side, e] = state
            state = decay * state + got[side, e]
        started = []
        for o in range(1, n_seq):
            copy = remote(
                out.at[side, peer[o]], in_ref.at[side, chunk(me), :], send.at[o], recv.at[o], {"seq": peer[o]}
            )
            copy.start()
            started.append(copy)
        in_ref[side, chunk(me), :] = out[side, me]
        return started

    group = poles // 2
    zero = jnp.zeros((SUB, LANES), F32)
    for h in range(nb // SUB):
        skip = skip_ref[h * SUB : (h + 1) * SUB, :]
        at = [pl.ds(n * nb + h * SUB, SUB) for n in range(poles)]
        for half in range(2):
            mine = at[half * group : (half + 1) * group]
            p = [p_ref[a, :] for a in mine]
            r = [r_ref[a, :] for a in mine]

            def forward(step, carry):
                s, acc, sk = carry
                s, acc = list(s), list(acc)
                for u in range(UNROLL):
                    rows = pl.ds(pl.multiple_of((step * UNROLL + u) * nb + h * SUB, SUB), SUB)
                    x, g = xs[rows, :], gs[rows, :]
                    terms = []
                    for n in range(group):
                        s[n] = p[n] * s[n] + x
                        acc[n] = acc[n] + g * s[n]
                        terms.append(r[n] * s[n])
                    while len(terms) > 1:
                        terms = [terms[i] + terms[i + 1] for i in range(0, len(terms), 2)]
                    if half == 0:
                        y_ref[rows, :] = terms[0] + skip * x
                        sk = sk + g * x
                    else:
                        y_ref[rows, :] = y_ref[rows, :] + terms[0]
                return tuple(s), tuple(acc), sk

            s, acc, sk = lax.fori_loop(
                0, length // UNROLL, forward, ((zero,) * group, (zero,) * group, zero)
            )
            for n in range(group):
                ends_ref[0, mine[n], :] = s[n]
                gr_ref[mine[n], :] = acc[n]
            if half == 0:
                gskip_ref[h * SUB : (h + 1) * SUB, :] = sk

    f_copies = send_ends(0, f_send, f_recv)
    for h in range(nb // SUB):
        if h == 1:
            f_copies = send_carries(0, f_copies, fb_send, fb_recv)
        skip = skip_ref[h * SUB : (h + 1) * SUB, :]
        at = [pl.ds(n * nb + h * SUB, SUB) for n in range(poles)]
        p = [p_ref[a, :] for a in at]
        r = [r_ref[a, :] for a in at]

        def backward(step, s):
            s = list(s)
            for u in range(UNROLL):
                t = length - 1 - (step * UNROLL + u)
                rows = pl.ds(pl.multiple_of(t * nb + h * SUB, SUB), SUB)
                g = gs[rows, :]
                terms = []
                for n in range(poles):
                    s[n] = p[n] * s[n] + g
                    terms.append(r[n] * s[n])
                while len(terms) > 1:
                    terms = [terms[i] + terms[i + 1] for i in range(0, len(terms), 2)]
                gm_ref[rows, :] = terms[0] + skip * g
            return tuple(s)

        s = lax.fori_loop(0, length // UNROLL, backward, (zero,) * poles)
        for n in range(poles):
            ends_ref[1, at[n], :] = s[n]
    a_copies = send_ends(1, a_send, a_recv)
    for copy in f_copies:
        copy.wait()

    def corrections(side, ref):
        for h in range(nb // SUB):
            at = [pl.ds(n * nb + h * SUB, SUB) for n in range(poles)]
            p = [p_ref[a, :] for a in at]

            def correct(step, u):
                u = list(u)
                for v in range(UNROLL):
                    t = step * UNROLL + v
                    t = length - 1 - t if side else t
                    rows = pl.ds(pl.multiple_of(t * nb + h * SUB, SUB), SUB)
                    parts = list(u)
                    while len(parts) > 1:
                        parts = [parts[i] + parts[i + 1] for i in range(0, len(parts), 2)]
                    ref[rows, :] = ref[rows, :] + parts[0]
                    u = [u[n] * p[n] for n in range(poles)]
                return tuple(u)

            lax.fori_loop(
                0, length // UNROLL, correct,
                tuple(r_ref[a, :] * (p_ref[a, :] * in_ref[side, a, :]) for a in at),
            )

    corrections(0, y_ref)
    a_copies = send_carries(1, a_copies, ab_send, ab_recv)
    terms[0:lines, :] = gr_ref[...] + in_ref[0] * p_ref[...] * ends_ref[1]
    terms[lines:first, :] = gskip_ref[...]
    if rows_used < terms.shape[0]:
        terms[rows_used:, :] = jnp.zeros((terms.shape[0] - rows_used, LANES), F32)
    hits_t = ot_ref[...]

    def emit(f, k, lanes, val, n4):
        val = val.astype(BF16)
        fg_ref[f, :, lanes] = val
        head_ref[f, :, lanes] = val[:SUB, :]
        sums = jnp.dot(hits_t, val, preferred_element_type=F32)
        taps = [jnp.sum(sums[i * SUB : (i + 1) * SUB, :] * n4, axis=0, keepdims=True) for i in range(TAPS)]
        terms[pl.ds(first + f * TAPS * nb + k, TAPS, stride=nb), :] = jnp.concatenate(taps, 0)

    def query_outputs(k, carry):
        lanes = pl.ds(pl.multiple_of(k * LANES, LANES), LANES)
        y = y_ref[pl.ds(k, length, stride=nb), :]
        hyena_ref[:, lanes] = (feat_ref[0, :, lanes].astype(F32) * y).astype(BF16)
        emit(0, k, lanes, ct_ref[:, lanes].astype(F32) * y, n4_ref[:, lanes])
        return carry

    lax.fori_loop(0, nb, query_outputs, 0)
    for copy in a_copies:
        copy.wait()
    corrections(1, gm_ref)

    def key_outputs(k, carry):
        lanes = pl.ds(pl.multiple_of(k * LANES, LANES), LANES)
        gm = gm_ref[pl.ds(k, length, stride=nb), :]
        n4 = n4_ref[:, lanes]
        emit(1, k, lanes, gm * feat_ref[2, :, lanes].astype(F32), n4)
        emit(2, k, lanes, gm * feat_ref[1, :, lanes].astype(F32), n4)
        return carry

    lax.fori_loop(0, nb, key_outputs, 0)
    terms_ref[...] = terms[...].astype(BF16)

    rt = terms_ref.shape[0] // n_seq
    part_at = lambda k: pl.ds(pl.multiple_of(k * rt, rt), rt)
    halo = remote(head_ref, tail, halo_sem.at[2], halo_sem.at[3], {"seq": peer[n_seq - 1]})
    halo.start()
    t_copies = []
    for o in range(1, n_seq):
        copy = remote(terms_ref.at[part_at(peer[o]), :], tgot.at[o], t_send.at[o], t_recv.at[o], {"seq": peer[o]})
        copy.start()
        t_copies.append(copy)
    keep = jnp.where(me < n_seq - 1, 1.0, 0.0).astype(F32)
    block = 64
    inner = length - block

    def filtered(k, begin, end, base):
        lanes = pl.ds(pl.multiple_of(k * LANES, LANES), LANES)
        w = [w_ref[f, i : i + 1, lanes] for f in range(3) for i in range(TAPS)]
        for b in range(begin, end, block):
            acc = jnp.zeros((block, LANES), F32)
            for f in range(3):
                for i in range(TAPS):
                    acc = acc + w[f * TAPS + i] * pad[f, b - base + i : b - base + i + block, :]
            gn_ref[b : b + block, lanes] = acc.astype(BF16)

    def inner_rows(k, carry):
        lanes = pl.ds(pl.multiple_of(k * LANES, LANES), LANES)
        for f in range(3):
            pad[f, 0:length, :] = fg_ref[f, :, lanes].astype(F32)
        filtered(k, 0, inner, 0)
        return carry

    def last_rows(k, carry):
        lanes = pl.ds(pl.multiple_of(k * LANES, LANES), LANES)
        for f in range(3):
            pad[f, 0:block, :] = fg_ref[f, inner:length, lanes].astype(F32)
            pad[f, block : block + SUB, :] = tail[f, :, lanes].astype(F32) * keep
        filtered(k, inner, length, inner)
        return carry

    lax.fori_loop(0, nb // 2, inner_rows, 0)
    summed = terms_ref[part_at(me), :].astype(F32)
    for o in range(1, n_seq):
        t_copies[o - 1].wait()
        summed = summed + tgot[o].astype(F32)
    total[...] = summed.astype(BF16)
    t_copies = []
    for o in range(1, n_seq):
        copy = remote(total, sums_ref.at[part_at(me), :], tb_send.at[o], tb_recv.at[o], {"seq": peer[o]})
        copy.start()
        t_copies.append(copy)
    sums_ref[part_at(me), :] = summed.astype(BF16)
    lax.fori_loop(nb // 2, nb, inner_rows, 0)
    halo.wait()
    lax.fori_loop(0, nb, last_rows, 0)
    for copy in t_copies:
        copy.wait()
    wide[...] = sums_ref[...].astype(F32)
    for k in range(nb):
        lanes = slice(k * LANES, (k + 1) * LANES)
        gr_out_ref[:, lanes] = wide[pl.ds(k, poles, stride=nb), :]
        gskip_out_ref[:, lanes] = wide[lines + k : lines + k + 1, :]
        for f in range(3):
            conv_ref[f, :, lanes] = wide[pl.ds(first + f * TAPS * nb + k, TAPS, stride=nb), :]


def finish_kernel(hyena_in, gn_in, conv_in, gr_in, gskip_in, hyena_ref, gn_ref, conv_ref, gr_ref, gskip_ref, sem):
    pairs = (
        (hyena_in, hyena_ref), (gn_in, gn_ref), (conv_in, conv_ref), (gr_in, gr_ref), (gskip_in, gskip_ref),
    )
    copies = [pltpu.make_async_copy(src, dst, sem.at[i]) for i, (src, dst) in enumerate(pairs)]
    for copy in copies:
        copy.start()
    for copy in copies:
        copy.wait()


def solution(mesh):
    n_seq, n_ch = mesh.shape["seq"], mesh.shape["ch"]
    dma = pltpu.SemaphoreType.DMA
    vmem = pltpu.VMEM

    def per_device(token_ids, embedding, norm_gain, conv_weight, pole_rates, residues, skip_gain, cotangent):
        length, chans = cotangent.shape
        poles = pole_rates.shape[0]
        nb = chans // LANES
        lines = poles * nb
        rp = lines // n_seq
        rows = lines + nb + 3 * TAPS * nb
        each = -(-rows // (16 * n_seq)) * 16
        tile = vmem((length * nb, LANES), F32)
        line = vmem((lines, LANES), F32)
        scratch = [
            vmem((1, length), jnp.int32), vmem((1, chans), F32), vmem((3, TAPS, chans), F32),
            vmem((poles, chans), F32), vmem((poles, chans), F32), vmem((1, chans), F32), vmem((length, chans), BF16),
            dma((7,)),
            vmem((SUB, LANES), F32), vmem((n_ch, SUB, LANES), F32), vmem((1, length), jnp.int32),
            vmem((3, length, chans), BF16), tile, tile, vmem((8 * SUB, length), BF16), vmem((SUB, chans), F32),
            vmem((2, lines, LANES), F32), vmem((2, lines, LANES), F32), line, vmem((nb, LANES), F32),
            line, line, line, vmem((nb, LANES), F32), tile, tile, vmem((3, 24 * SUB, chans), BF16),
            vmem((2, n_seq, rp, LANES), F32), vmem((2, n_seq, rp, LANES), F32),
            vmem((3, length, chans), BF16), vmem((3, SUB, chans), BF16), vmem((3, SUB, chans), BF16),
            vmem((each * n_seq, LANES), F32), vmem((each * n_seq, LANES), BF16),
            vmem((n_seq, each, LANES), BF16), vmem((each, LANES), BF16), vmem((each * n_seq, LANES), BF16),
            vmem((each * n_seq, LANES), F32), vmem((3, length + SUB, LANES), F32),
            vmem((BAND, chans), BF16), dma, dma((n_ch,)), dma((n_ch,)), dma((4,)),
        ] + [dma((n_seq,))] * 12
        outs = [
            ((length, chans), BF16), ((length, chans), BF16), ((3, TAPS, chans), F32), ((poles, chans), F32),
            ((1, chans), F32),
        ]
        ins = (
            token_ids.reshape(1, length), embedding, norm_gain.reshape(1, chans), conv_weight, pole_rates, residues,
            skip_gain.reshape(1, chans), cotangent,
        )
        held = pl.pallas_call(
            functools.partial(mega_kernel, n_seq, n_ch, poles),
            out_shape=[pltpu.VMEM(shape, dtype) for shape, dtype in outs],
            in_specs=[
                pl.BlockSpec(memory_space=pl.ANY) for i in range(len(ins))
            ],
            out_specs=[pl.BlockSpec(memory_space=pltpu.VMEM)] * len(outs),
            scratch_shapes=scratch,
            compiler_params=pltpu.CompilerParams(
                vmem_limit_bytes=VLIMIT, collective_id=0, has_side_effects=True
            ),
        )(*ins)
        hyena, grad_normed, conv, gr, gskip = pl.pallas_call(
            finish_kernel,
            out_shape=[jax.ShapeDtypeStruct(shape, dtype) for shape, dtype in outs],
            in_specs=[pl.BlockSpec(memory_space=pltpu.VMEM)] * len(outs),
            out_specs=[pl.BlockSpec(memory_space=pl.ANY)] * len(outs),
            scratch_shapes=[dma((len(outs),))],
        )(*(pltpu.with_memory_space_constraint(part, pltpu.VMEM) for part in held))
        return hyena, grad_normed, conv, gr, gskip.reshape(chans)

    in_specs = (
        P("seq"), P(None, "ch"), P("ch"), P(None, None, "ch"), P(None, "ch"), P(None, "ch"), P("ch"), P("seq", "ch"),
    )
    out_specs = (P("seq", "ch"), P("seq", "ch"), P(None, None, "ch"), P(None, "ch"), P("ch"))
    return jax.shard_map(per_device, mesh=mesh, in_specs=in_specs, out_specs=out_specs, check_vma=False)
```

```python
import functools

import jax
import jax.numpy as jnp
from jax import lax
from jax.experimental import pallas as pl
from jax.experimental.pallas import tpu as pltpu
from jax.sharding import PartitionSpec as P

TAPS = 7
CODES = (65, 67, 71, 84)
MESH = pl.DeviceIdType.MESH
F32 = jnp.float32
BF16 = jnp.bfloat16
LANES = 128
SUB = 8
CHUNK = 8
GAP = 8
PAIR = 2
BAND = 32
VLIMIT = 60 * 1024 * 1024


def greet(peers):
    barrier = pltpu.get_barrier_semaphore()
    for peer in peers:
        pl.semaphore_signal(barrier, inc=1, device_id=peer, device_id_type=MESH)


def greeted(peers):
    pl.semaphore_wait(pltpu.get_barrier_semaphore(), len(peers))


def remote(src, dst, send_sem, recv_sem, peer):
    return pltpu.make_async_remote_copy(
        src_ref=src, dst_ref=dst, send_sem=send_sem, recv_sem=recv_sem,
        device_id=peer, device_id_type=MESH,
    )


def mega_kernel(
    n_seq, n_ch, poles,
    ids_in, emb_ref, gain_in, w_in, rate_in, res_in, skip_in, ct_in,
    hyena_ref, gn_ref, conv_ref, gr_out_ref, gskip_out_ref,
    ids_ref, gain_ref, w_ref, rate_ref, res_ref, skip_in_ref, ct_ref, load_sem,
    part, ss_got, prev_got, feat_ref, y_ref, gm_ref, ot_ref, n4_ref, ends_ref, in_ref, gr_ref, gskip_ref,
    p_ref, rp_ref, pc_ref, hs_ref, lag_ref, s0_ref, b0_ref, decay_ref, xs, gs, table, got, out, fg_ref, head_ref, tail,
    terms_e, whole_e, tgot_e, total_e, sums_e, wide_e, terms_l, whole_l, tgot_l, total_l, sums_l, wide_l, pad,
    emb_rows, emb_sem, ss_send, ss_recv, halo_sem, f_send, f_recv, fb_send, fb_recv, a_send, a_recv, ab_send, ab_recv,
    t_send, t_recv, tb_send, tb_recv, l_send, l_recv, lb_send, lb_recv,
):
    me = lax.axis_index("seq")
    ch = lax.axis_index("ch")
    length, chans = ct_ref.shape
    width = chans * n_ch
    nb = chans // LANES
    pitch = nb + GAP
    lines = poles * nb
    first = lines + nb
    peer = [lax.rem(me + o, n_seq) for o in range(n_seq)]
    ch_peer = [lax.rem(ch + o, n_ch) for o in range(n_ch)]

    peers = [{"seq": peer[o]} for o in range(1, n_seq)] + [{"ch": ch_peer[o]} for o in range(1, n_ch)]
    greet(peers)
    low_row = min(CODES) // BAND * BAND
    fetch = pltpu.make_async_copy(emb_ref.at[low_row : low_row + BAND, :], emb_rows, emb_sem)
    fetch.start()
    loads = [
        pltpu.make_async_copy(src, dst, load_sem.at[i])
        for i, (src, dst) in enumerate((
            (rate_in, rate_ref), (res_in, res_ref), (skip_in, skip_in_ref), (ids_in, ids_ref), (gain_in, gain_ref),
            (w_in, w_ref), (ct_in, ct_ref),
        ))
    ]
    for load in loads:
        load.start()
    for load in loads[:3]:
        load.wait()
    for k in range(nb):
        lanes = slice(k * LANES, (k + 1) * LANES)
        rates = rate_ref[:, lanes]
        rows = pl.ds(k, poles, stride=nb)
        p_ref[rows, :] = jnp.exp(-rates)
        decay_ref[rows, :] = jnp.exp(-rates * length)
        pc_ref[rows, :] = jnp.exp(-rates * CHUNK)
        rp_ref[rows, :] = res_ref[:, lanes] * jnp.exp(-rates)
        weight = res_ref[:, lanes]
        for d in range(CHUNK):
            tap = jnp.sum(weight, axis=0, keepdims=True)
            hs_ref[d * nb + k : d * nb + k + 1, :] = tap + skip_in_ref[:, lanes] if d == 0 else tap
            weight = weight * jnp.exp(-rates)
    fetch.wait()
    emb = jnp.concatenate(
        [emb_rows[v - low_row : v - low_row + 1, :].astype(F32) for v in CODES]
        + [jnp.zeros((SUB - len(CODES), chans), F32)],
        0,
    )
    squares = jnp.broadcast_to(jnp.sum(emb * emb, axis=1, keepdims=True), (SUB, LANES))
    part[...] = squares
    greeted(peers)
    ids_copy = remote(ids_in, prev_got, halo_sem.at[0], halo_sem.at[1], {"seq": peer[1]})
    ids_copy.start()
    copies = []
    for o in range(1, n_ch):
        copy = remote(part, ss_got.at[o], ss_send.at[o], ss_recv.at[o], {"ch": ch_peer[o]})
        copy.start()
        copies.append(copy)
    for load in loads[3:6]:
        load.wait()
    ids_copy.wait()
    prev = jnp.where(me > 0, prev_got[...], -1)
    row = lax.broadcasted_iota(jnp.int32, (SUB, length), 0)
    code = jnp.full((SUB, length), -2, jnp.int32)
    for a, value in enumerate(CODES):
        code = jnp.where(row == a, value, code)
    ext = jnp.concatenate([prev, ids_ref[...]], 1)
    hits = [
        jnp.where(ext[:, length - i : 2 * length - i] == code, 1.0, 0.0).astype(F32) for i in range(TAPS)
    ] + [jnp.zeros((SUB, length), F32)]
    onehot = jnp.concatenate(hits, 0)
    ot_ref[...] = onehot.astype(BF16)
    picks = jnp.transpose(jnp.concatenate([onehot] * 2, 0)).astype(BF16)
    for o in range(1, n_ch):
        copies[o - 1].wait()
        squares = squares + ss_got[o]
    scale = lax.rsqrt(squares / width + 1e-05)[:, :1]
    n4 = (emb * scale * gain_ref[...]).astype(BF16).astype(F32)
    n4_ref[...] = n4
    zero_rows = jnp.zeros((SUB, chans), F32)
    for f in range(3):
        full = jnp.concatenate(
            [w_ref[f, i : i + 1, :] * n4 for i in range(TAPS)] + [zero_rows], 0
        )
        high = full.astype(BF16)
        rest = full - high.astype(F32)
        table[f, 0 : 8 * SUB, :] = high
        table[f, 8 * SUB : 16 * SUB, :] = rest.astype(BF16)

    def features(kb, carry):
        lanes = pl.ds(pl.multiple_of(kb * 256, 256), 256)
        parts = []
        for f in range(3):
            val = jnp.dot(picks, table[f, :, lanes], preferred_element_type=F32).astype(BF16)
            feat_ref[f, :, lanes] = val
            parts.append(val.astype(F32))
        x = parts[1] * parts[2]
        g = ct_ref[:, lanes].astype(F32) * parts[0]
        for s in range(2):
            xs[pl.ds(kb * 2 + s, length, stride=pitch), :] = x[:, s * LANES : (s + 1) * LANES]
            gs[pl.ds(kb * 2 + s, length, stride=pitch), :] = g[:, s * LANES : (s + 1) * LANES]
        return carry

    loads[6].wait()
    lax.fori_loop(0, chans // 256, features, 0)


    rp = lines // n_seq
    chunk = lambda k: pl.ds(pl.multiple_of(k * rp, rp), rp)

    def send_ends(side, send, recv):
        started = []
        for o in range(1, n_seq):
            copy = remote(
                ends_ref.at[side, chunk(peer[o]), :], got.at[side, me], send.at[o], recv.at[o], {"seq": peer[o]}
            )
            copy.start()
            started.append(copy)
        got[side, me] = ends_ref[side, chunk(me), :]
        return started

    def send_carries(side, started, send, recv):
        for copy in started:
            copy.wait()
        decay = decay_ref[chunk(me), :]
        state = jnp.zeros_like(decay)
        for e in reversed(range(n_seq)) if side else range(n_seq):
            out[side, e] = state
            state = decay * state + got[side, e]
        started = []
        for o in range(1, n_seq):
            copy = remote(
                out.at[side, peer[o]], in_ref.at[side, chunk(me), :], send.at[o], recv.at[o], {"seq": peer[o]}
            )
            copy.start()
            started.append(copy)
        in_ref[side, chunk(me), :] = out[side, me]
        return started

    group = poles // 2
    zero = jnp.zeros((SUB, LANES), F32)
    halves = range(nb // SUB)
    chunks = length // CHUNK
    at = [[pl.ds(n * nb + h * SUB, SUB) for n in range(poles)] for h in halves]

    def row(ref_row, h):
        return pl.ds(pl.multiple_of(ref_row * nb + h * SUB, SUB), SUB)

    def time(t, h):
        return pl.ds(pl.multiple_of(t * pitch + h * SUB, SUB), SUB)

    def tree(values):
        values = list(values)
        while len(values) > 1:
            values = [
                values[i] + values[i + 1] if i + 1 < len(values) else values[i] for i in range(0, len(values), 2)
            ]
        return values[0]

    for h in halves:
        for half in range(2):
            poles_of = range(half * group, (half + 1) * group)
            p = [p_ref[at[h][n], :] for n in poles_of]
            pc = [pc_ref[at[h][n], :] for n in poles_of]

            def states(step, s):
                s = list(s)
                for c in range(PAIR):
                    u = step * PAIR + c
                    for i, n in enumerate(poles_of):
                        s0_ref[row(u * poles + n, h), :] = s[i]
                    for v in range(CHUNK):
                        x = xs[time(u * CHUNK + v, h), :]
                        e = [p[i] * e[i] + x for i in range(group)] if v else [x] * group
                    s = [pc[i] * s[i] + e[i] for i in range(group)]
                return tuple(s)

            s = lax.fori_loop(0, chunks // PAIR, states, (zero,) * group)
            for i, n in enumerate(poles_of):
                ends_ref[0, at[h][n], :] = s[i]

    f_copies = send_ends(0, f_send, f_recv)
    for h in halves:
        for half in range(2):
            poles_of = range(half * group, (half + 1) * group)
            p = [p_ref[at[h][n], :] for n in poles_of]
            pc = [pc_ref[at[h][n], :] for n in poles_of]

            def adjoints(step, carry):
                s, acc = list(carry[0]), list(carry[1])
                for c in range(PAIR):
                    u = chunks - 1 - (step * PAIR + c)
                    for i, n in enumerate(poles_of):
                        b0_ref[row(u * poles + n, h), :] = s[i]
                    for v in reversed(range(CHUNK)):
                        g = gs[time(u * CHUNK + v, h), :]
                        e = [p[i] * e[i] + g for i in range(group)] if v < CHUNK - 1 else [g] * group
                    s = [pc[i] * s[i] + e[i] for i in range(group)]
                    acc = [acc[i] + s0_ref[row(u * poles + n, h), :] * e[i] for i, n in enumerate(poles_of)]
                return tuple(s), tuple(acc)

            s, acc = lax.fori_loop(0, chunks // PAIR, adjoints, ((zero,) * group, (zero,) * group))
            for i, n in enumerate(poles_of):
                ends_ref[1, at[h][n], :] = s[i]
                gr_ref[at[h][n], :] = acc[i]
    f_copies = send_carries(0, f_copies, fb_send, fb_recv)
    a_copies = send_ends(1, a_send, a_recv)

    for h in halves:
        taps = [hs_ref[row(d, h), :] for d in range(CHUNK)]

        def near(u, lag):
            lag = list(lag)
            x = [xs[time(u * CHUNK + v, h), :] for v in range(CHUNK)]
            g = [gs[time(u * CHUNK + v, h), :] for v in range(CHUNK)]
            for v in range(CHUNK):
                y_ref[time(u * CHUNK + v, h), :] = tree(taps[d] * x[v - d] for d in range(v + 1))
                gm_ref[time(u * CHUNK + v, h), :] = tree(taps[d] * g[v + d] for d in range(CHUNK - v))
            for d in range(CHUNK):
                lag[d] = lag[d] + tree(g[v + d] * x[v] for v in range(CHUNK - d))
            return tuple(lag)

        lag = lax.fori_loop(0, chunks, near, (zero,) * CHUNK)
        gskip_ref[h * SUB : (h + 1) * SUB, :] = lag[0]
        for n in range(poles):
            p = p_ref[at[h][n], :]
            total_lag = lag[CHUNK - 1]
            for d in reversed(range(CHUNK - 1)):
                total_lag = p * total_lag + lag[d]
            lag_ref[at[h][n], :] = total_lag
    for copy in f_copies:
        copy.wait()
    a_copies = send_carries(1, a_copies, ab_send, ab_recv)

    def far(side, kept, ref):
        for h in halves:
            p = [p_ref[at[h][n], :] for n in range(poles)]

            def readout(step, w):
                u = chunks - 1 - step if side else step
                part = [rp_ref[at[h][n], :] * kept[row(u * poles + n, h), :] + w[n] for n in range(poles)]
                for v in reversed(range(CHUNK)) if side else range(CHUNK):
                    rows = time(u * CHUNK + v, h)
                    ref[rows, :] = ref[rows, :] + tree(part)
                    part = [part[n] * p[n] for n in range(poles)]
                return tuple(w[n] * pc_ref[at[h][n], :] for n in range(poles))

            lax.fori_loop(0, chunks, readout, tuple(rp_ref[a, :] * in_ref[side, a, :] for a in at[h]))

    far(0, s0_ref, y_ref)
    terms_e[0:lines, :] = p_ref[...] * (gr_ref[...] + in_ref[0] * ends_ref[1]) + lag_ref[...]
    terms_e[lines:first, :] = gskip_ref[...]
    for ref, used in ((terms_e, first + TAPS * nb), (terms_l, 2 * TAPS * nb)):
        if used < ref.shape[0]:
            ref[used:, :] = jnp.zeros((ref.shape[0] - used, LANES), F32)
    hits_t = ot_ref[...]
    wide_lanes = 2 * LANES

    def emit(f, k, lanes, val, ref, base):
        val = val.astype(BF16)
        fg_ref[f, :, lanes] = val
        head_ref[f, :, lanes] = val[:SUB, :]
        sums = jnp.dot(hits_t, val, preferred_element_type=F32)
        n4 = n4_ref[:, lanes]
        taps = jnp.concatenate(
            [jnp.sum(sums[i * SUB : (i + 1) * SUB, :] * n4, axis=0, keepdims=True) for i in range(TAPS)], 0
        )
        for s in range(2):
            ref[pl.ds(base + k * 2 + s, TAPS, stride=nb), :] = taps[:, s * LANES : (s + 1) * LANES]

    def along(ref, k):
        return jnp.concatenate([ref[pl.ds(k * 2 + s, length, stride=pitch), :] for s in range(2)], 1)

    def query_outputs(k, carry):
        lanes = pl.ds(pl.multiple_of(k * wide_lanes, wide_lanes), wide_lanes)
        y = along(y_ref, k)
        hyena_ref[:, lanes] = (feat_ref[0, :, lanes].astype(F32) * y).astype(BF16)
        emit(0, k, lanes, ct_ref[:, lanes].astype(F32) * y, terms_e, first)
        return carry

    def scatter(whole, ref, got_ref, send, recv):
        whole[...] = ref[...].astype(BF16)
        rows = whole.shape[0] // n_seq
        started = []
        for o in range(1, n_seq):
            mine = pl.ds(pl.multiple_of(peer[o] * rows, rows), rows)
            copy = remote(whole.at[mine, :], got_ref.at[o], send.at[o], recv.at[o], {"seq": peer[o]})
            copy.start()
            started.append(copy)
        return started

    def gather(started, whole, got_ref, total, sums, send, recv):
        rows = whole.shape[0] // n_seq
        mine = pl.ds(pl.multiple_of(me * rows, rows), rows)
        summed = whole[mine, :].astype(F32)
        for o in range(1, n_seq):
            started[o - 1].wait()
            summed = summed + got_ref[o].astype(F32)
        total[...] = summed.astype(BF16)
        started = []
        for o in range(1, n_seq):
            copy = remote(total, sums.at[mine, :], send.at[o], recv.at[o], {"seq": peer[o]})
            copy.start()
            started.append(copy)
        sums[mine, :] = summed.astype(BF16)
        return started

    lax.fori_loop(0, nb // 2, query_outputs, 0)
    e_copies = scatter(whole_e, terms_e, tgot_e, t_send, t_recv)
    for copy in a_copies:
        copy.wait()
    far(1, b0_ref, gm_ref)
    e_copies = gather(e_copies, whole_e, tgot_e, total_e, sums_e, tb_send, tb_recv)

    def key_outputs(k, carry):
        lanes = pl.ds(pl.multiple_of(k * wide_lanes, wide_lanes), wide_lanes)
        gm = along(gm_ref, k)
        emit(1, k, lanes, gm * feat_ref[2, :, lanes].astype(F32), terms_l, 0)
        emit(2, k, lanes, gm * feat_ref[1, :, lanes].astype(F32), terms_l, TAPS * nb)
        return carry

    lax.fori_loop(0, nb // 2, key_outputs, 0)
    l_copies = scatter(whole_l, terms_l, tgot_l, l_send, l_recv)
    halo = remote(head_ref, tail, halo_sem.at[2], halo_sem.at[3], {"seq": peer[n_seq - 1]})
    halo.start()
    keep = jnp.where(me < n_seq - 1, 1.0, 0.0).astype(F32)
    block = 64
    inner = length - block

    def filtered(k, begin, end, base):
        lanes = pl.ds(pl.multiple_of(k * LANES, LANES), LANES)
        w = [w_ref[f, i : i + 1, lanes] for f in range(3) for i in range(TAPS)]
        for b in range(begin, end, block):
            acc = jnp.zeros((block, LANES), F32)
            for f in range(3):
                for i in range(TAPS):
                    acc = acc + w[f * TAPS + i] * pad[f, b - base + i : b - base + i + block, :]
            gn_ref[b : b + block, lanes] = acc.astype(BF16)

    def inner_rows(k, carry):
        lanes = pl.ds(pl.multiple_of(k * LANES, LANES), LANES)
        for f in range(3):
            pad[f, 0:length, :] = fg_ref[f, :, lanes].astype(F32)
        filtered(k, 0, inner, 0)
        return carry

    def last_rows(k, carry):
        lanes = pl.ds(pl.multiple_of(k * LANES, LANES), LANES)
        for f in range(3):
            pad[f, 0:block, :] = fg_ref[f, inner:length, lanes].astype(F32)
            pad[f, block : block + SUB, :] = tail[f, :, lanes].astype(F32) * keep
        filtered(k, inner, length, inner)
        return carry

    lax.fori_loop(0, nb // 2, inner_rows, 0)
    l_copies = gather(l_copies, whole_l, tgot_l, total_l, sums_l, lb_send, lb_recv)
    lax.fori_loop(nb // 2, nb, inner_rows, 0)
    for copy in e_copies:
        copy.wait()
    wide_e[...] = sums_e[...].astype(F32)
    for k in range(nb):
        lanes = slice(k * LANES, (k + 1) * LANES)
        gr_out_ref[:, lanes] = wide_e[pl.ds(k, poles, stride=nb), :]
        gskip_out_ref[:, lanes] = wide_e[lines + k : lines + k + 1, :]
        conv_ref[0, :, lanes] = wide_e[pl.ds(first + k, TAPS, stride=nb), :]
    halo.wait()
    lax.fori_loop(0, nb, last_rows, 0)
    for copy in l_copies:
        copy.wait()
    wide_l[...] = sums_l[...].astype(F32)
    for k in range(nb):
        lanes = slice(k * LANES, (k + 1) * LANES)
        for f in range(1, 3):
            conv_ref[f, :, lanes] = wide_l[pl.ds((f - 1) * TAPS * nb + k, TAPS, stride=nb), :]


def finish_kernel(hyena_in, gn_in, conv_in, gr_in, gskip_in, hyena_ref, gn_ref, conv_ref, gr_ref, gskip_ref, sem):
    pairs = (
        (hyena_in, hyena_ref), (gn_in, gn_ref), (conv_in, conv_ref), (gr_in, gr_ref), (gskip_in, gskip_ref),
    )
    copies = [pltpu.make_async_copy(src, dst, sem.at[i]) for i, (src, dst) in enumerate(pairs)]
    for copy in copies:
        copy.start()
    for copy in copies:
        copy.wait()


def solution(mesh):
    n_seq, n_ch = mesh.shape["seq"], mesh.shape["ch"]
    dma = pltpu.SemaphoreType.DMA
    vmem = pltpu.VMEM

    def per_device(token_ids, embedding, norm_gain, conv_weight, pole_rates, residues, skip_gain, cotangent):
        length, chans = cotangent.shape
        poles = pole_rates.shape[0]
        nb = chans // LANES
        lines = poles * nb
        rp = lines // n_seq

        def reduced(rows):
            each = -(-rows // (16 * n_seq)) * 16
            return [
                vmem((each * n_seq, LANES), F32), vmem((each * n_seq, LANES), BF16), vmem((n_seq, each, LANES), BF16),
                vmem((each, LANES), BF16), vmem((each * n_seq, LANES), BF16), vmem((each * n_seq, LANES), F32),
            ]

        tile = vmem((length * (nb + GAP), LANES), F32)
        line = vmem((lines, LANES), F32)
        kept = vmem((length // CHUNK * lines, LANES), F32)
        scratch = [
            vmem((1, length), jnp.int32), vmem((1, chans), F32), vmem((3, TAPS, chans), F32),
            vmem((poles, chans), F32), vmem((poles, chans), F32), vmem((1, chans), F32), vmem((length, chans), BF16),
            dma((7,)),
            vmem((SUB, LANES), F32), vmem((n_ch, SUB, LANES), F32), vmem((1, length), jnp.int32),
            vmem((3, length, chans), BF16), tile, tile, vmem((8 * SUB, length), BF16), vmem((SUB, chans), F32),
            vmem((2, lines, LANES), F32), vmem((2, lines, LANES), F32), line, vmem((nb, LANES), F32),
            line, line, line, vmem((CHUNK * nb, LANES), F32), line, kept, kept, line, tile, tile, vmem((3, 16 * SUB, chans), BF16),
            vmem((2, n_seq, rp, LANES), F32), vmem((2, n_seq, rp, LANES), F32),
            vmem((3, length, chans), BF16), vmem((3, SUB, chans), BF16), vmem((3, SUB, chans), BF16),
            *reduced(lines + nb + TAPS * nb), *reduced(2 * TAPS * nb), vmem((3, length + SUB, LANES), F32),
            vmem((BAND, chans), BF16), dma, dma((n_ch,)), dma((n_ch,)), dma((4,)),
        ] + [dma((n_seq,))] * 16
        outs = [
            ((length, chans), BF16), ((length, chans), BF16), ((3, TAPS, chans), F32), ((poles, chans), F32),
            ((1, chans), F32),
        ]
        ins = (
            token_ids.reshape(1, length), embedding, norm_gain.reshape(1, chans), conv_weight, pole_rates, residues,
            skip_gain.reshape(1, chans), cotangent,
        )
        held = pl.pallas_call(
            functools.partial(mega_kernel, n_seq, n_ch, poles),
            out_shape=[pltpu.VMEM(shape, dtype) for shape, dtype in outs],
            in_specs=[
                pl.BlockSpec(memory_space=pl.ANY) for i in range(len(ins))
            ],
            out_specs=[pl.BlockSpec(memory_space=pltpu.VMEM)] * len(outs),
            scratch_shapes=scratch,
            compiler_params=pltpu.CompilerParams(
                vmem_limit_bytes=VLIMIT, collective_id=0, has_side_effects=True
            ),
        )(*ins)
        hyena, grad_normed, conv, gr, gskip = pl.pallas_call(
            finish_kernel,
            out_shape=[jax.ShapeDtypeStruct(shape, dtype) for shape, dtype in outs],
            in_specs=[pl.BlockSpec(memory_space=pltpu.VMEM)] * len(outs),
            out_specs=[pl.BlockSpec(memory_space=pl.ANY)] * len(outs),
            scratch_shapes=[dma((len(outs),))],
        )(*(pltpu.with_memory_space_constraint(part, pltpu.VMEM) for part in held))
        return hyena, grad_normed, conv, gr, gskip.reshape(chans)

    in_specs = (
        P("seq"), P(None, "ch"), P("ch"), P(None, None, "ch"), P(None, "ch"), P(None, "ch"), P("ch"), P("seq", "ch"),
    )
    out_specs = (P("seq", "ch"), P("seq", "ch"), P(None, None, "ch"), P(None, "ch"), P("ch"))
    return jax.shard_map(per_device, mesh=mesh, in_specs=in_specs, out_specs=out_specs, check_vma=False)
```

```python
import functools

import jax
import jax.numpy as jnp
from jax import lax
from jax.experimental import pallas as pl
from jax.experimental.pallas import tpu as pltpu
from jax.sharding import PartitionSpec as P

TAPS = 7
CODES = (65, 67, 71, 84)
MESH = pl.DeviceIdType.MESH
F32 = jnp.float32
BF16 = jnp.bfloat16
LANES = 128
SUB = 8
CHUNK = 8
GAP = 8
PAIR = 2
BAND = 32
VLIMIT = 60 * 1024 * 1024


def greet(peers):
    barrier = pltpu.get_barrier_semaphore()
    for peer in peers:
        pl.semaphore_signal(barrier, inc=1, device_id=peer, device_id_type=MESH)


def greeted(peers):
    pl.semaphore_wait(pltpu.get_barrier_semaphore(), len(peers))


def remote(src, dst, send_sem, recv_sem, peer):
    return pltpu.make_async_remote_copy(
        src_ref=src, dst_ref=dst, send_sem=send_sem, recv_sem=recv_sem,
        device_id=peer, device_id_type=MESH,
    )


def mega_kernel(
    n_seq, n_ch, poles,
    ids_in, emb_ref, gain_in, w_in, rate_in, res_in, skip_in, ct_in,
    hyena_ref, gn_ref, conv_ref, gr_out_ref, gskip_out_ref,
    ids_ref, gain_ref, w_ref, rate_ref, res_ref, skip_in_ref, ct_ref, load_sem,
    part, ss_got, prev_got, feat_ref, y_ref, gm_ref, ot_ref, n4_ref, ends_ref, in_ref, gr_ref, gskip_ref,
    p_ref, rp_ref, pc_ref, hs_ref, lag_ref, s0_ref, b0_ref, decay_ref, xs, gs, table, got, out, fg_ref, head_ref, tail,
    terms_e, whole_e, tgot_e, total_e, sums_e, wide_e, terms_l, whole_l, tgot_l, total_l, sums_l, wide_l, pad,
    emb_rows, emb_sem, ss_send, ss_recv, halo_sem, x_send, x_recv, xb_send, xb_recv,
    t_send, t_recv, tb_send, tb_recv, l_send, l_recv, lb_send, lb_recv,
):
    me = lax.axis_index("seq")
    ch = lax.axis_index("ch")
    length, chans = ct_ref.shape
    width = chans * n_ch
    nb = chans // LANES
    pitch = nb + GAP
    lines = poles * nb
    first = lines + nb
    peer = [lax.rem(me + o, n_seq) for o in range(n_seq)]
    ch_peer = [lax.rem(ch + o, n_ch) for o in range(n_ch)]

    peers = [{"seq": peer[o]} for o in range(1, n_seq)] + [{"ch": ch_peer[o]} for o in range(1, n_ch)]
    greet(peers)
    low_row = min(CODES) // BAND * BAND
    fetch = pltpu.make_async_copy(emb_ref.at[low_row : low_row + BAND, :], emb_rows, emb_sem)
    fetch.start()
    loads = [
        pltpu.make_async_copy(src, dst, load_sem.at[i])
        for i, (src, dst) in enumerate((
            (rate_in, rate_ref), (res_in, res_ref), (skip_in, skip_in_ref), (ids_in, ids_ref), (gain_in, gain_ref),
            (w_in, w_ref), (ct_in, ct_ref),
        ))
    ]
    for load in loads:
        load.start()
    for load in loads[:3]:
        load.wait()
    for k in range(nb):
        lanes = slice(k * LANES, (k + 1) * LANES)
        rates = rate_ref[:, lanes]
        rows = pl.ds(k // SUB * poles * SUB + k % SUB, poles, stride=SUB)
        p_ref[rows, :] = jnp.exp(-rates)
        decay_ref[rows, :] = jnp.exp(-rates * length)
        pc_ref[rows, :] = jnp.exp(-rates * CHUNK)
        rp_ref[rows, :] = res_ref[:, lanes] * jnp.exp(-rates)
        weight = res_ref[:, lanes]
        for d in range(CHUNK):
            tap = jnp.sum(weight, axis=0, keepdims=True)
            hs_ref[d * nb + k : d * nb + k + 1, :] = tap + skip_in_ref[:, lanes] if d == 0 else tap
            weight = weight * jnp.exp(-rates)
    fetch.wait()
    emb = jnp.concatenate(
        [emb_rows[v - low_row : v - low_row + 1, :].astype(F32) for v in CODES]
        + [jnp.zeros((SUB - len(CODES), chans), F32)],
        0,
    )
    squares = jnp.broadcast_to(jnp.sum(emb * emb, axis=1, keepdims=True), (SUB, LANES))
    part[...] = squares
    greeted(peers)
    ids_copy = remote(ids_in, prev_got, halo_sem.at[0], halo_sem.at[1], {"seq": peer[1]})
    ids_copy.start()
    copies = []
    for o in range(1, n_ch):
        copy = remote(part, ss_got.at[o], ss_send.at[o], ss_recv.at[o], {"ch": ch_peer[o]})
        copy.start()
        copies.append(copy)
    for load in loads[3:6]:
        load.wait()
    ids_copy.wait()
    prev = jnp.where(me > 0, prev_got[...], -1)
    row = lax.broadcasted_iota(jnp.int32, (SUB, length), 0)
    code = jnp.full((SUB, length), -2, jnp.int32)
    for a, value in enumerate(CODES):
        code = jnp.where(row == a, value, code)
    ext = jnp.concatenate([prev, ids_ref[...]], 1)
    hits = [
        jnp.where(ext[:, length - i : 2 * length - i] == code, 1.0, 0.0).astype(F32) for i in range(TAPS)
    ] + [jnp.zeros((SUB, length), F32)]
    onehot = jnp.concatenate(hits, 0)
    ot_ref[...] = onehot.astype(BF16)
    picks = jnp.transpose(jnp.concatenate([onehot] * 2, 0)).astype(BF16)
    for o in range(1, n_ch):
        copies[o - 1].wait()
        squares = squares + ss_got[o]
    scale = lax.rsqrt(squares / width + 1e-05)[:, :1]
    n4 = (emb * scale * gain_ref[...]).astype(BF16).astype(F32)
    n4_ref[...] = n4
    zero_rows = jnp.zeros((SUB, chans), F32)
    for f in range(3):
        full = jnp.concatenate(
            [w_ref[f, i : i + 1, :] * n4 for i in range(TAPS)] + [zero_rows], 0
        )
        high = full.astype(BF16)
        rest = full - high.astype(F32)
        table[f, 0 : 8 * SUB, :] = high
        table[f, 8 * SUB : 16 * SUB, :] = rest.astype(BF16)

    def feature_block(kb):
        lanes = pl.ds(pl.multiple_of(kb * 256, 256), 256)
        parts = []
        for f in range(3):
            val = jnp.dot(picks, table[f, :, lanes], preferred_element_type=F32).astype(BF16)
            feat_ref[f, :, lanes] = val
            parts.append(val.astype(F32))
        x = parts[1] * parts[2]
        g = ct_ref[:, lanes].astype(F32) * parts[0]
        for s in range(2):
            xs[pl.ds(kb * 2 + s, length, stride=pitch), :] = x[:, s * LANES : (s + 1) * LANES]
            gs[pl.ds(kb * 2 + s, length, stride=pitch), :] = g[:, s * LANES : (s + 1) * LANES]

    def features(step, carry):
        for b in range(2):
            feature_block(step * 2 + b)
        return carry

    loads[6].wait()
    lax.fori_loop(0, chans // 512, features, 0)


    own = min(n_seq, poles)
    held = poles * SUB
    rp = held // own
    base = me // own * own
    back = [base + lax.rem(me - base + o, own) for o in range(own)]

    def chunk(k, h):
        return pl.ds(pl.multiple_of(h * held + lax.rem(k, own) * rp, rp), rp)

    def send_ends(side, h):
        started = []
        for o in range(1, n_seq):
            copy = remote(
                ends_ref.at[side, chunk(peer[o], h), :], got.at[side, h, me],
                x_send.at[side, h, o], x_recv.at[side, h, o], {"seq": peer[o]},
            )
            copy.start()
            started.append(copy)
        got[side, h, me] = ends_ref[side, chunk(me, h), :]
        return started

    def send_carries(side, h, started):
        for copy in started:
            copy.wait()
        decay = decay_ref[chunk(me, h), :]
        state = jnp.zeros_like(decay)
        for e in reversed(range(n_seq)) if side else range(n_seq):
            out[side, h, e] = state
            state = decay * state + got[side, h, e]
        started = []
        for o in range(1, own):
            copy = remote(
                out.at[side, h, back[o]], in_ref.at[side, chunk(me, h), :],
                xb_send.at[side, h, o], xb_recv.at[side, h, o], {"seq": back[o]},
            )
            copy.start()
            started.append(copy)
        in_ref[side, chunk(me, h), :] = out[side, h, me]
        return started

    group = poles // 2
    zero = jnp.zeros((SUB, LANES), F32)
    halves = range(nb // SUB)
    chunks = length // CHUNK
    at = [[pl.ds((h * poles + n) * SUB, SUB) for n in range(poles)] for h in halves]

    def row(ref_row, h):
        return pl.ds(pl.multiple_of(ref_row * nb + h * SUB, SUB), SUB)

    def time(t, h):
        return pl.ds(pl.multiple_of(t * pitch + h * SUB, SUB), SUB)

    def tree(values):
        values = list(values)
        while len(values) > 1:
            values = [
                values[i] + values[i + 1] if i + 1 < len(values) else values[i] for i in range(0, len(values), 2)
            ]
        return values[0]

    f_copies = []
    for h in halves:
        for half in range(2):
            poles_of = range(half * group, (half + 1) * group)
            p = [p_ref[at[h][n], :] for n in poles_of]
            pc = [pc_ref[at[h][n], :] for n in poles_of]

            def states(step, s):
                s = list(s)
                for c in range(PAIR):
                    u = step * PAIR + c
                    for i, n in enumerate(poles_of):
                        s0_ref[row(u * poles + n, h), :] = s[i]
                    for v in range(CHUNK):
                        x = xs[time(u * CHUNK + v, h), :]
                        e = [p[i] * e[i] + x for i in range(group)] if v else [x] * group
                    s = [pc[i] * s[i] + e[i] for i in range(group)]
                return tuple(s)

            s = lax.fori_loop(0, chunks // PAIR, states, (zero,) * group)
            for i, n in enumerate(poles_of):
                ends_ref[0, at[h][n], :] = s[i]
        f_copies.append(send_ends(0, h))

    a_copies = []
    for h in halves:
        for half in range(2):
            poles_of = range(half * group, (half + 1) * group)
            p = [p_ref[at[h][n], :] for n in poles_of]
            pc = [pc_ref[at[h][n], :] for n in poles_of]

            def adjoints(step, carry):
                s, acc = list(carry[0]), list(carry[1])
                for c in range(PAIR):
                    u = chunks - 1 - (step * PAIR + c)
                    for i, n in enumerate(poles_of):
                        b0_ref[row(u * poles + n, h), :] = s[i]
                    for v in reversed(range(CHUNK)):
                        g = gs[time(u * CHUNK + v, h), :]
                        e = [p[i] * e[i] + g for i in range(group)] if v < CHUNK - 1 else [g] * group
                    s = [pc[i] * s[i] + e[i] for i in range(group)]
                    acc = [acc[i] + s0_ref[row(u * poles + n, h), :] * e[i] for i, n in enumerate(poles_of)]
                return tuple(s), tuple(acc)

            s, acc = lax.fori_loop(0, chunks // PAIR, adjoints, ((zero,) * group, (zero,) * group))
            for i, n in enumerate(poles_of):
                ends_ref[1, at[h][n], :] = s[i]
                gr_ref[at[h][n], :] = acc[i]
        f_copies[h] = send_carries(0, h, f_copies[h])
        a_copies.append(send_ends(1, h))

    for h in halves:
        taps = [hs_ref[row(d, h), :] for d in range(CHUNK)]

        def near(u, lag):
            lag = list(lag)
            x = [xs[time(u * CHUNK + v, h), :] for v in range(CHUNK)]
            g = [gs[time(u * CHUNK + v, h), :] for v in range(CHUNK)]
            for v in range(CHUNK):
                y_ref[time(u * CHUNK + v, h), :] = tree(taps[d] * x[v - d] for d in range(v + 1))
                gm_ref[time(u * CHUNK + v, h), :] = tree(taps[d] * g[v + d] for d in range(CHUNK - v))
            for d in range(CHUNK):
                lag[d] = lag[d] + tree(g[v + d] * x[v] for v in range(CHUNK - d))
            return tuple(lag)

        lag = lax.fori_loop(0, chunks, near, (zero,) * CHUNK)
        gskip_ref[h * SUB : (h + 1) * SUB, :] = lag[0]
        for n in range(poles):
            p = p_ref[at[h][n], :]
            total_lag = lag[CHUNK - 1]
            for d in reversed(range(CHUNK - 1)):
                total_lag = p * total_lag + lag[d]
            lag_ref[at[h][n], :] = total_lag

    def far(side, h, started, kept, ref):
        for copy in started:
            copy.wait()
        p = [p_ref[at[h][n], :] for n in range(poles)]

        def readout(step, w):
            u = chunks - 1 - step if side else step
            part = [rp_ref[at[h][n], :] * kept[row(u * poles + n, h), :] + w[n] for n in range(poles)]
            for v in reversed(range(CHUNK)) if side else range(CHUNK):
                rows = time(u * CHUNK + v, h)
                ref[rows, :] = ref[rows, :] + tree(part)
                part = [part[n] * p[n] for n in range(poles)]
            return tuple(w[n] * pc_ref[at[h][n], :] for n in range(poles))

        lax.fori_loop(0, chunks, readout, tuple(rp_ref[a, :] * in_ref[side, a, :] for a in at[h]))

    for h in halves:
        a_copies[h] = send_carries(1, h, a_copies[h])
        far(0, h, f_copies[h], s0_ref, y_ref)
    terms_e[0:lines, :] = p_ref[...] * (gr_ref[...] + in_ref[0] * ends_ref[1]) + lag_ref[...]
    terms_e[lines:first, :] = gskip_ref[...]
    for ref, used in ((terms_e, first + TAPS * nb), (terms_l, 2 * TAPS * nb)):
        if used < ref.shape[0]:
            ref[used:, :] = jnp.zeros((ref.shape[0] - used, LANES), F32)
    hits_t = ot_ref[...]
    wide_lanes = 2 * LANES

    def emit(f, k, lanes, val, ref, base):
        val = val.astype(BF16)
        fg_ref[f, :, lanes] = val
        head_ref[f, :, lanes] = val[:SUB, :]
        sums = jnp.dot(hits_t, val, preferred_element_type=F32)
        n4 = n4_ref[:, lanes]
        taps = jnp.concatenate(
            [jnp.sum(sums[i * SUB : (i + 1) * SUB, :] * n4, axis=0, keepdims=True) for i in range(TAPS)], 0
        )
        for s in range(2):
            ref[pl.ds(base + k * 2 + s, TAPS, stride=nb), :] = taps[:, s * LANES : (s + 1) * LANES]

    def along(ref, k):
        return jnp.concatenate([ref[pl.ds(k * 2 + s, length, stride=pitch), :] for s in range(2)], 1)

    def query_outputs_block(k):
        lanes = pl.ds(pl.multiple_of(k * wide_lanes, wide_lanes), wide_lanes)
        y = along(y_ref, k)
        emit(0, k, lanes, ct_ref[:, lanes].astype(F32) * y, terms_e, first)

    def query_outputs(step, carry):
        for b in range(2):
            query_outputs_block(step * 2 + b)
        return carry

    def scatter(whole, ref, got_ref, send, recv):
        whole[...] = ref[...].astype(BF16)
        rows = whole.shape[0] // n_seq
        started = []
        for o in range(1, n_seq):
            mine = pl.ds(pl.multiple_of(peer[o] * rows, rows), rows)
            copy = remote(whole.at[mine, :], got_ref.at[o], send.at[o], recv.at[o], {"seq": peer[o]})
            copy.start()
            started.append(copy)
        return started

    def gather(started, whole, got_ref, total, sums, send, recv):
        rows = whole.shape[0] // n_seq
        mine = pl.ds(pl.multiple_of(me * rows, rows), rows)
        summed = whole[mine, :].astype(F32)
        for o in range(1, n_seq):
            started[o - 1].wait()
            summed = summed + got_ref[o].astype(F32)
        total[...] = summed.astype(BF16)
        started = []
        for o in range(1, n_seq):
            copy = remote(total, sums.at[mine, :], send.at[o], recv.at[o], {"seq": peer[o]})
            copy.start()
            started.append(copy)
        sums[mine, :] = summed.astype(BF16)
        return started

    lax.fori_loop(0, nb // 4, query_outputs, 0)
    e_copies = scatter(whole_e, terms_e, tgot_e, t_send, t_recv)
    for h in halves:
        far(1, h, a_copies[h], b0_ref, gm_ref)
        if h == 0:
            e_copies = gather(e_copies, whole_e, tgot_e, total_e, sums_e, tb_send, tb_recv)

    def key_outputs_block(k):
        lanes = pl.ds(pl.multiple_of(k * wide_lanes, wide_lanes), wide_lanes)
        gm = along(gm_ref, k)
        emit(1, k, lanes, gm * feat_ref[2, :, lanes].astype(F32), terms_l, 0)
        emit(2, k, lanes, gm * feat_ref[1, :, lanes].astype(F32), terms_l, TAPS * nb)

    def key_outputs(step, carry):
        for b in range(2):
            key_outputs_block(step * 2 + b)
        return carry

    lax.fori_loop(0, nb // 4, key_outputs, 0)
    l_copies = scatter(whole_l, terms_l, tgot_l, l_send, l_recv)
    halo = remote(head_ref, tail, halo_sem.at[2], halo_sem.at[3], {"seq": peer[n_seq - 1]})
    halo.start()
    keep = jnp.where(me < n_seq - 1, 1.0, 0.0).astype(F32)
    block = 64
    inner = length - block

    def filtered(k, begin, end, base):
        lanes = pl.ds(pl.multiple_of(k * LANES, LANES), LANES)
        w = [w_ref[f, i : i + 1, lanes] for f in range(3) for i in range(TAPS)]
        for b in range(begin, end, block):
            acc = jnp.zeros((block, LANES), F32)
            for f in range(3):
                for i in range(TAPS):
                    acc = acc + w[f * TAPS + i] * pad[f, b - base + i : b - base + i + block, :]
            gn_ref[b : b + block, lanes] = acc.astype(BF16)

    def inner_rows(k, carry):
        lanes = pl.ds(pl.multiple_of(k * LANES, LANES), LANES)
        for f in range(3):
            pad[f, 0:length, :] = fg_ref[f, :, lanes].astype(F32)
        filtered(k, 0, inner, 0)
        return carry

    def last_rows(k, carry):
        lanes = pl.ds(pl.multiple_of(k * LANES, LANES), LANES)
        for f in range(3):
            pad[f, 0:block, :] = fg_ref[f, inner:length, lanes].astype(F32)
            pad[f, block : block + SUB, :] = tail[f, :, lanes].astype(F32) * keep
        filtered(k, inner, length, inner)
        return carry

    def hyena_rows(k, carry):
        lanes = pl.ds(pl.multiple_of(k * wide_lanes, wide_lanes), wide_lanes)
        hyena_ref[:, lanes] = (feat_ref[0, :, lanes].astype(F32) * along(y_ref, k)).astype(BF16)
        return carry

    lax.fori_loop(0, nb // 2, hyena_rows, 0)
    lax.fori_loop(0, 3 * nb // 4, inner_rows, 0)
    l_copies = gather(l_copies, whole_l, tgot_l, total_l, sums_l, lb_send, lb_recv)
    lax.fori_loop(3 * nb // 4, nb, inner_rows, 0)
    for copy in e_copies:
        copy.wait()
    wide_e[...] = sums_e[...].astype(F32)
    for k in range(nb):
        lanes = slice(k * LANES, (k + 1) * LANES)
        gr_out_ref[:, lanes] = wide_e[pl.ds(k // SUB * poles * SUB + k % SUB, poles, stride=SUB), :]
        gskip_out_ref[:, lanes] = wide_e[lines + k : lines + k + 1, :]
        conv_ref[0, :, lanes] = wide_e[pl.ds(first + k, TAPS, stride=nb), :]
    halo.wait()
    lax.fori_loop(0, nb, last_rows, 0)
    for copy in l_copies:
        copy.wait()
    wide_l[...] = sums_l[...].astype(F32)
    for k in range(nb):
        lanes = slice(k * LANES, (k + 1) * LANES)
        for f in range(1, 3):
            conv_ref[f, :, lanes] = wide_l[pl.ds((f - 1) * TAPS * nb + k, TAPS, stride=nb), :]


def finish_kernel(hyena_in, gn_in, conv_in, gr_in, gskip_in, hyena_ref, gn_ref, conv_ref, gr_ref, gskip_ref, sem):
    pairs = (
        (hyena_in, hyena_ref), (gn_in, gn_ref), (conv_in, conv_ref), (gr_in, gr_ref), (gskip_in, gskip_ref),
    )
    copies = [pltpu.make_async_copy(src, dst, sem.at[i]) for i, (src, dst) in enumerate(pairs)]
    for copy in copies:
        copy.start()
    for copy in copies:
        copy.wait()


def solution(mesh):
    n_seq, n_ch = mesh.shape["seq"], mesh.shape["ch"]
    dma = pltpu.SemaphoreType.DMA
    vmem = pltpu.VMEM

    def per_device(token_ids, embedding, norm_gain, conv_weight, pole_rates, residues, skip_gain, cotangent):
        length, chans = cotangent.shape
        poles = pole_rates.shape[0]
        nb = chans // LANES
        lines = poles * nb
        rp = poles * SUB // min(n_seq, poles)

        def reduced(rows):
            each = -(-rows // (16 * n_seq)) * 16
            return [
                vmem((each * n_seq, LANES), F32), vmem((each * n_seq, LANES), BF16), vmem((n_seq, each, LANES), BF16),
                vmem((each, LANES), BF16), vmem((each * n_seq, LANES), BF16), vmem((each * n_seq, LANES), F32),
            ]

        tile = vmem((length * (nb + GAP), LANES), F32)
        line = vmem((lines, LANES), F32)
        kept = vmem((length // CHUNK * lines, LANES), F32)
        scratch = [
            vmem((1, length), jnp.int32), vmem((1, chans), F32), vmem((3, TAPS, chans), F32),
            vmem((poles, chans), F32), vmem((poles, chans), F32), vmem((1, chans), F32), vmem((length, chans), BF16),
            dma((7,)),
            vmem((SUB, LANES), F32), vmem((n_ch, SUB, LANES), F32), vmem((1, length), jnp.int32),
            vmem((3, length, chans), BF16), tile, tile, vmem((8 * SUB, length), BF16), vmem((SUB, chans), F32),
            vmem((2, lines, LANES), F32), vmem((2, lines, LANES), F32), line, vmem((nb, LANES), F32),
            line, line, line, vmem((CHUNK * nb, LANES), F32), line, kept, kept, line, tile, tile, vmem((3, 16 * SUB, chans), BF16),
            vmem((2, nb // SUB, n_seq, rp, LANES), F32), vmem((2, nb // SUB, n_seq, rp, LANES), F32),
            vmem((3, length, chans), BF16), vmem((3, SUB, chans), BF16), vmem((3, SUB, chans), BF16),
            *reduced(lines + nb + TAPS * nb), *reduced(2 * TAPS * nb), vmem((3, length + SUB, LANES), F32),
            vmem((BAND, chans), BF16), dma, dma((n_ch,)), dma((n_ch,)), dma((4,)),
        ] + [dma((2, nb // SUB, n_seq))] * 4 + [dma((n_seq,))] * 8
        outs = [
            ((length, chans), BF16), ((length, chans), BF16), ((3, TAPS, chans), F32), ((poles, chans), F32),
            ((1, chans), F32),
        ]
        ins = (
            token_ids.reshape(1, length), embedding, norm_gain.reshape(1, chans), conv_weight, pole_rates, residues,
            skip_gain.reshape(1, chans), cotangent,
        )
        held = pl.pallas_call(
            functools.partial(mega_kernel, n_seq, n_ch, poles),
            out_shape=[pltpu.VMEM(shape, dtype) for shape, dtype in outs],
            in_specs=[
                pl.BlockSpec(memory_space=pl.ANY) for i in range(len(ins))
            ],
            out_specs=[pl.BlockSpec(memory_space=pltpu.VMEM)] * len(outs),
            scratch_shapes=scratch,
            compiler_params=pltpu.CompilerParams(
                vmem_limit_bytes=VLIMIT, collective_id=0, has_side_effects=True
            ),
        )(*ins)
        hyena, grad_normed, conv, gr, gskip = pl.pallas_call(
            finish_kernel,
            out_shape=[jax.ShapeDtypeStruct(shape, dtype) for shape, dtype in outs],
            in_specs=[pl.BlockSpec(memory_space=pltpu.VMEM)] * len(outs),
            out_specs=[pl.BlockSpec(memory_space=pl.ANY)] * len(outs),
            scratch_shapes=[dma((len(outs),))],
        )(*(pltpu.with_memory_space_constraint(part, pltpu.VMEM) for part in held))
        return hyena, grad_normed, conv, gr, gskip.reshape(chans)

    in_specs = (
        P("seq"), P(None, "ch"), P("ch"), P(None, None, "ch"), P(None, "ch"), P(None, "ch"), P("ch"), P("seq", "ch"),
    )
    out_specs = (P("seq", "ch"), P("seq", "ch"), P(None, None, "ch"), P(None, "ch"), P("ch"))
    return jax.shard_map(per_device, mesh=mesh, in_specs=in_specs, out_specs=out_specs, check_vma=False)
```

```python
import functools

import jax
import jax.numpy as jnp
from jax import lax
from jax.experimental import pallas as pl
from jax.experimental.pallas import tpu as pltpu
from jax.sharding import PartitionSpec as P

TAPS = 7
CODES = (65, 67, 71, 84)
MESH = pl.DeviceIdType.MESH
F32 = jnp.float32
BF16 = jnp.bfloat16
LANES = 128
SUB = 8
CHUNK = 8
GAP = 8
PAIR = 2
BAND = 32
VLIMIT = 60 * 1024 * 1024


def greet(peers):
    barrier = pltpu.get_barrier_semaphore()
    for peer in peers:
        pl.semaphore_signal(barrier, inc=1, device_id=peer, device_id_type=MESH)


def greeted(peers):
    pl.semaphore_wait(pltpu.get_barrier_semaphore(), len(peers))


def remote(src, dst, send_sem, recv_sem, peer):
    return pltpu.make_async_remote_copy(
        src_ref=src, dst_ref=dst, send_sem=send_sem, recv_sem=recv_sem,
        device_id=peer, device_id_type=MESH,
    )


def mega_kernel(
    n_seq, n_ch, poles,
    ids_in, emb_ref, gain_in, w_in, rate_in, res_in, skip_in, ct_in,
    hyena_ref, gn_ref, conv_ref, gr_out_ref, gskip_out_ref,
    ids_ref, gain_ref, w_ref, rate_ref, res_ref, skip_in_ref, ct_ref, load_sem,
    part, ss_got, prev_got, feat_ref, y_ref, gm_ref, ot_ref, n4_ref, ends_ref, in_ref, gr_ref, gskip_ref,
    p_ref, rp_ref, pc_ref, hs_ref, lag_ref, s0_ref, b0_ref, decay_ref, xs, gs, table, got, out, fg_ref, head_ref, tail,
    terms_e, whole_e, tgot_e, total_e, sums_e, wide_e, terms_l, whole_l, tgot_l, total_l, sums_l, wide_l, pad,
    emb_rows, emb_sem, ss_send, ss_recv, halo_sem, x_send, x_recv, xb_send, xb_recv,
    t_send, t_recv, tb_send, tb_recv, l_send, l_recv, lb_send, lb_recv,
):
    me = lax.axis_index("seq")
    ch = lax.axis_index("ch")
    length, chans = ct_ref.shape
    width = chans * n_ch
    nb = chans // LANES
    pitch = nb + GAP
    lines = poles * nb
    first = lines + nb
    peer = [lax.rem(me + o, n_seq) for o in range(n_seq)]
    ch_peer = [lax.rem(ch + o, n_ch) for o in range(n_ch)]

    peers = [{"seq": peer[o]} for o in range(1, n_seq)] + [{"ch": ch_peer[o]} for o in range(1, n_ch)]
    greet(peers)
    low_row = min(CODES) // BAND * BAND
    fetch = pltpu.make_async_copy(emb_ref.at[low_row : low_row + BAND, :], emb_rows, emb_sem)
    fetch.start()
    loads = [
        pltpu.make_async_copy(src, dst, load_sem.at[i])
        for i, (src, dst) in enumerate((
            (rate_in, rate_ref), (res_in, res_ref), (skip_in, skip_in_ref), (ids_in, ids_ref), (gain_in, gain_ref),
            (w_in, w_ref), (ct_in, ct_ref),
        ))
    ]
    for load in loads:
        load.start()
    for load in loads[:3]:
        load.wait()
    for k in range(nb):
        lanes = slice(k * LANES, (k + 1) * LANES)
        rates = rate_ref[:, lanes]
        rows = pl.ds(k // SUB * poles * SUB + k % SUB, poles, stride=SUB)
        p_ref[rows, :] = jnp.exp(-rates)
        decay_ref[rows, :] = jnp.exp(-rates * length)
        pc_ref[rows, :] = jnp.exp(-rates * CHUNK)
        rp_ref[rows, :] = res_ref[:, lanes] * jnp.exp(-rates)
        weight = res_ref[:, lanes]
        for d in range(CHUNK):
            tap = jnp.sum(weight, axis=0, keepdims=True)
            hs_ref[d * nb + k : d * nb + k + 1, :] = tap + skip_in_ref[:, lanes] if d == 0 else tap
            weight = weight * jnp.exp(-rates)
    fetch.wait()
    emb = jnp.concatenate(
        [emb_rows[v - low_row : v - low_row + 1, :].astype(F32) for v in CODES] * 2,
        0,
    )
    squares = jnp.broadcast_to(jnp.sum(emb * emb, axis=1, keepdims=True), (SUB, LANES))
    part[...] = squares
    greeted(peers)
    ids_copy = remote(ids_in, prev_got, halo_sem.at[0], halo_sem.at[1], {"seq": peer[1]})
    ids_copy.start()
    copies = []
    for o in range(1, n_ch):
        copy = remote(part, ss_got.at[o], ss_send.at[o], ss_recv.at[o], {"ch": ch_peer[o]})
        copy.start()
        copies.append(copy)
    for load in loads[3:6]:
        load.wait()
    ids_copy.wait()
    prev = jnp.where(me > 0, prev_got[...], -1)
    row = lax.broadcasted_iota(jnp.int32, (SUB, length), 0)
    code = jnp.full((SUB, length), -2, jnp.int32)
    for a, value in enumerate(CODES):
        code = jnp.where(lax.rem(row, len(CODES)) == a, value, code)
    ext = jnp.concatenate([prev, ids_ref[...]], 1)
    shifted = [ext[:, length - i : 2 * length - i] for i in range(TAPS)] + [jnp.full((1, length), -1, jnp.int32)]
    hits = [
        jnp.where(jnp.where(row >= len(CODES), shifted[2 * j + 1], shifted[2 * j]) == code, 1.0, 0.0).astype(F32)
        for j in range(SUB // 2)
    ]
    onehot = jnp.concatenate(hits, 0)
    ot_ref[...] = onehot.astype(BF16)
    picks = jnp.transpose(jnp.concatenate([onehot] * 2, 0)).astype(BF16)
    for o in range(1, n_ch):
        copies[o - 1].wait()
        squares = squares + ss_got[o]
    scale = lax.rsqrt(squares / width + 1e-05)[:, :1]
    n4 = (emb * scale * gain_ref[...]).astype(BF16).astype(F32)
    n4_ref[...] = n4
    later = lax.broadcasted_iota(jnp.int32, (SUB, chans), 0) >= len(CODES)
    for f in range(3):
        w = [w_ref[f, i : i + 1, :] for i in range(TAPS)] + [jnp.zeros((1, chans), F32)]
        full = jnp.concatenate([jnp.where(later, w[2 * j + 1], w[2 * j]) * n4 for j in range(SUB // 2)], 0)
        high = full.astype(BF16)
        rest = full - high.astype(F32)
        table[f, 0 : 4 * SUB, :] = high
        table[f, 4 * SUB : 8 * SUB, :] = rest.astype(BF16)

    def feature_block(kb):
        lanes = pl.ds(pl.multiple_of(kb * 256, 256), 256)
        parts = []
        for f in range(3):
            val = jnp.dot(picks, table[f, :, lanes], preferred_element_type=F32).astype(BF16)
            feat_ref[f, :, lanes] = val
            parts.append(val.astype(F32))
        x = parts[1] * parts[2]
        g = ct_ref[:, lanes].astype(F32) * parts[0]
        for s in range(2):
            xs[pl.ds(kb * 2 + s, length, stride=pitch), :] = x[:, s * LANES : (s + 1) * LANES]
            gs[pl.ds(kb * 2 + s, length, stride=pitch), :] = g[:, s * LANES : (s + 1) * LANES]

    def features(step, carry):
        for b in range(2):
            feature_block(step * 2 + b)
        return carry

    loads[6].wait()
    lax.fori_loop(0, chans // 512, features, 0)


    own = min(n_seq, poles)
    held = poles * SUB
    rp = held // own
    base = me // own * own
    back = [base + lax.rem(me - base + o, own) for o in range(own)]

    def chunk(k, h):
        return pl.ds(pl.multiple_of(h * held + lax.rem(k, own) * rp, rp), rp)

    def send_ends(side, h):
        started = []
        for o in range(1, n_seq):
            copy = remote(
                ends_ref.at[side, chunk(peer[o], h), :], got.at[side, h, me],
                x_send.at[side, h, o], x_recv.at[side, h, o], {"seq": peer[o]},
            )
            copy.start()
            started.append(copy)
        got[side, h, me] = ends_ref[side, chunk(me, h), :]
        return started

    def send_carries(side, h, started):
        for copy in started:
            copy.wait()
        decay = decay_ref[chunk(me, h), :]
        state = jnp.zeros_like(decay)
        for e in reversed(range(n_seq)) if side else range(n_seq):
            out[side, h, e] = state
            state = decay * state + got[side, h, e]
        started = []
        for o in range(1, own):
            copy = remote(
                out.at[side, h, back[o]], in_ref.at[side, chunk(me, h), :],
                xb_send.at[side, h, o], xb_recv.at[side, h, o], {"seq": back[o]},
            )
            copy.start()
            started.append(copy)
        in_ref[side, chunk(me, h), :] = out[side, h, me]
        return started

    group = poles // 2
    zero = jnp.zeros((SUB, LANES), F32)
    halves = range(nb // SUB)
    chunks = length // CHUNK
    at = [[pl.ds((h * poles + n) * SUB, SUB) for n in range(poles)] for h in halves]

    def row(ref_row, h):
        return pl.ds(pl.multiple_of(ref_row * nb + h * SUB, SUB), SUB)

    def time(t, h):
        return pl.ds(pl.multiple_of(t * pitch + h * SUB, SUB), SUB)

    def tree(values):
        values = list(values)
        while len(values) > 1:
            values = [
                values[i] + values[i + 1] if i + 1 < len(values) else values[i] for i in range(0, len(values), 2)
            ]
        return values[0]

    f_copies = []
    for h in halves:
        for half in range(2):
            poles_of = range(half * group, (half + 1) * group)
            p = [p_ref[at[h][n], :] for n in poles_of]
            pc = [pc_ref[at[h][n], :] for n in poles_of]

            def states(step, s):
                s = list(s)
                for c in range(PAIR):
                    u = step * PAIR + c
                    for i, n in enumerate(poles_of):
                        s0_ref[row(u * poles + n, h), :] = s[i]
                    for v in range(CHUNK):
                        x = xs[time(u * CHUNK + v, h), :]
                        e = [p[i] * e[i] + x for i in range(group)] if v else [x] * group
                    s = [pc[i] * s[i] + e[i] for i in range(group)]
                return tuple(s)

            s = lax.fori_loop(0, chunks // PAIR, states, (zero,) * group)
            for i, n in enumerate(poles_of):
                ends_ref[0, at[h][n], :] = s[i]
        f_copies.append(send_ends(0, h))

    a_copies = []
    for h in halves:
        for half in range(2):
            poles_of = range(half * group, (half + 1) * group)
            p = [p_ref[at[h][n], :] for n in poles_of]
            pc = [pc_ref[at[h][n], :] for n in poles_of]

            def adjoints(step, carry):
                s, acc = list(carry[0]), list(carry[1])
                for c in range(PAIR):
                    u = chunks - 1 - (step * PAIR + c)
                    for i, n in enumerate(poles_of):
                        b0_ref[row(u * poles + n, h), :] = s[i]
                    for v in reversed(range(CHUNK)):
                        g = gs[time(u * CHUNK + v, h), :]
                        e = [p[i] * e[i] + g for i in range(group)] if v < CHUNK - 1 else [g] * group
                    s = [pc[i] * s[i] + e[i] for i in range(group)]
                    acc = [acc[i] + s0_ref[row(u * poles + n, h), :] * e[i] for i, n in enumerate(poles_of)]
                return tuple(s), tuple(acc)

            s, acc = lax.fori_loop(0, chunks // PAIR, adjoints, ((zero,) * group, (zero,) * group))
            for i, n in enumerate(poles_of):
                ends_ref[1, at[h][n], :] = s[i]
                gr_ref[at[h][n], :] = acc[i]
        f_copies[h] = send_carries(0, h, f_copies[h])
        a_copies.append(send_ends(1, h))

    for h in halves:
        taps = [hs_ref[row(d, h), :] for d in range(CHUNK)]

        def near_chunk(u, lag):
            lag = list(lag)
            x = [xs[time(u * CHUNK + v, h), :] for v in range(CHUNK)]
            g = [gs[time(u * CHUNK + v, h), :] for v in range(CHUNK)]
            for v in range(CHUNK):
                y_ref[time(u * CHUNK + v, h), :] = tree(taps[d] * x[v - d] for d in range(v + 1))
                gm_ref[time(u * CHUNK + v, h), :] = tree(taps[d] * g[v + d] for d in range(CHUNK - v))
            for d in range(CHUNK):
                lag[d] = lag[d] + tree(g[v + d] * x[v] for v in range(CHUNK - d))
            return tuple(lag)

        def near(step, lag):
            for c in range(PAIR):
                lag = near_chunk(step * PAIR + c, lag)
            return lag

        lag = lax.fori_loop(0, chunks // PAIR, near, (zero,) * CHUNK)
        gskip_ref[h * SUB : (h + 1) * SUB, :] = lag[0]
        for n in range(poles):
            p = p_ref[at[h][n], :]
            total_lag = lag[CHUNK - 1]
            for d in reversed(range(CHUNK - 1)):
                total_lag = p * total_lag + lag[d]
            lag_ref[at[h][n], :] = total_lag

    def far(side, h, started, kept, ref):
        for copy in started:
            copy.wait()
        p = [p_ref[at[h][n], :] for n in range(poles)]

        def readout_chunk(step, w):
            u = chunks - 1 - step if side else step
            part = [rp_ref[at[h][n], :] * kept[row(u * poles + n, h), :] + w[n] for n in range(poles)]
            for v in reversed(range(CHUNK)) if side else range(CHUNK):
                rows = time(u * CHUNK + v, h)
                ref[rows, :] = ref[rows, :] + tree(part)
                part = [part[n] * p[n] for n in range(poles)]
            return tuple(w[n] * pc_ref[at[h][n], :] for n in range(poles))

        def readout(step, w):
            for c in range(PAIR):
                w = readout_chunk(step * PAIR + c, w)
            return w

        lax.fori_loop(0, chunks // PAIR, readout, tuple(rp_ref[a, :] * in_ref[side, a, :] for a in at[h]))

    for h in halves:
        a_copies[h] = send_carries(1, h, a_copies[h])
        far(0, h, f_copies[h], s0_ref, y_ref)
    terms_e[0:lines, :] = p_ref[...] * (gr_ref[...] + in_ref[0] * ends_ref[1]) + lag_ref[...]
    terms_e[lines:first, :] = gskip_ref[...]
    for ref, used in ((terms_e, first + TAPS * nb), (terms_l, 2 * TAPS * nb)):
        if used < ref.shape[0]:
            ref[used:, :] = jnp.zeros((ref.shape[0] - used, LANES), F32)
    hits_t = ot_ref[...]
    wide_lanes = 2 * LANES

    def emit(f, k, lanes, val, ref, base):
        val = val.astype(BF16)
        fg_ref[f, :, lanes] = val
        head_ref[f, :, lanes] = val[:SUB, :]
        sums = jnp.dot(hits_t, val, preferred_element_type=F32)
        n4 = n4_ref[:, lanes]
        taps = []
        for i in range(SUB // 2):
            pair = sums[i * SUB : (i + 1) * SUB, :] * n4
            pair = pair + pltpu.roll(pair, 2, 0)
            pair = pair + pltpu.roll(pair, 1, 0)
            taps += [pair[len(CODES) - 1 : len(CODES), :], pair[SUB - 1 : SUB, :]]
        taps = jnp.concatenate(taps[:TAPS], 0)
        for s in range(2):
            ref[pl.ds(base + k * 2 + s, TAPS, stride=nb), :] = taps[:, s * LANES : (s + 1) * LANES]

    def along(ref, k):
        return jnp.concatenate([ref[pl.ds(k * 2 + s, length, stride=pitch), :] for s in range(2)], 1)

    def query_outputs_block(k):
        lanes = pl.ds(pl.multiple_of(k * wide_lanes, wide_lanes), wide_lanes)
        y = along(y_ref, k)
        emit(0, k, lanes, ct_ref[:, lanes].astype(F32) * y, terms_e, first)

    def query_outputs(step, carry):
        for b in range(2):
            query_outputs_block(step * 2 + b)
        return carry

    def scatter(whole, ref, got_ref, send, recv):
        whole[...] = ref[...].astype(BF16)
        rows = whole.shape[0] // n_seq
        started = []
        for o in range(1, n_seq):
            mine = pl.ds(pl.multiple_of(peer[o] * rows, rows), rows)
            copy = remote(whole.at[mine, :], got_ref.at[o], send.at[o], recv.at[o], {"seq": peer[o]})
            copy.start()
            started.append(copy)
        return started

    def gather(started, whole, got_ref, total, sums, send, recv):
        rows = whole.shape[0] // n_seq
        mine = pl.ds(pl.multiple_of(me * rows, rows), rows)
        summed = whole[mine, :].astype(F32)
        for o in range(1, n_seq):
            started[o - 1].wait()
            summed = summed + got_ref[o].astype(F32)
        total[...] = summed.astype(BF16)
        started = []
        for o in range(1, n_seq):
            copy = remote(total, sums.at[mine, :], send.at[o], recv.at[o], {"seq": peer[o]})
            copy.start()
            started.append(copy)
        sums[mine, :] = summed.astype(BF16)
        return started

    lax.fori_loop(0, nb // 4, query_outputs, 0)
    e_copies = scatter(whole_e, terms_e, tgot_e, t_send, t_recv)
    for h in halves:
        far(1, h, a_copies[h], b0_ref, gm_ref)
        if h == 0:
            e_copies = gather(e_copies, whole_e, tgot_e, total_e, sums_e, tb_send, tb_recv)

    def key_outputs_block(k):
        lanes = pl.ds(pl.multiple_of(k * wide_lanes, wide_lanes), wide_lanes)
        gm = along(gm_ref, k)
        emit(1, k, lanes, gm * feat_ref[2, :, lanes].astype(F32), terms_l, 0)
        emit(2, k, lanes, gm * feat_ref[1, :, lanes].astype(F32), terms_l, TAPS * nb)

    def key_outputs(step, carry):
        for b in range(2):
            key_outputs_block(step * 2 + b)
        return carry

    lax.fori_loop(0, nb // 4, key_outputs, 0)
    l_copies = scatter(whole_l, terms_l, tgot_l, l_send, l_recv)
    halo = remote(head_ref, tail, halo_sem.at[2], halo_sem.at[3], {"seq": peer[n_seq - 1]})
    halo.start()
    keep = jnp.where(me < n_seq - 1, 1.0, 0.0).astype(F32)
    block = 64
    inner = length - block

    def filtered(k, begin, end, base):
        lanes = pl.ds(pl.multiple_of(k * LANES, LANES), LANES)
        w = [w_ref[f, i : i + 1, lanes] for f in range(3) for i in range(TAPS)]
        for b in range(begin, end, block):
            acc = jnp.zeros((block, LANES), F32)
            for f in range(3):
                for i in range(TAPS):
                    acc = acc + w[f * TAPS + i] * pad[f, b - base + i : b - base + i + block, :]
            gn_ref[b : b + block, lanes] = acc.astype(BF16)

    def inner_rows(k, carry):
        lanes = pl.ds(pl.multiple_of(k * LANES, LANES), LANES)
        for f in range(3):
            pad[f, 0:length, :] = fg_ref[f, :, lanes].astype(F32)
        filtered(k, 0, inner, 0)
        return carry

    def last_rows(k, carry):
        lanes = pl.ds(pl.multiple_of(k * LANES, LANES), LANES)
        for f in range(3):
            pad[f, 0:block, :] = fg_ref[f, inner:length, lanes].astype(F32)
            pad[f, block : block + SUB, :] = tail[f, :, lanes].astype(F32) * keep
        filtered(k, inner, length, inner)
        return carry

    def hyena_rows(k, carry):
        lanes = pl.ds(pl.multiple_of(k * wide_lanes, wide_lanes), wide_lanes)
        hyena_ref[:, lanes] = (feat_ref[0, :, lanes].astype(F32) * along(y_ref, k)).astype(BF16)
        return carry

    lax.fori_loop(0, nb // 2, hyena_rows, 0)
    lax.fori_loop(0, 3 * nb // 4, inner_rows, 0)
    l_copies = gather(l_copies, whole_l, tgot_l, total_l, sums_l, lb_send, lb_recv)
    lax.fori_loop(3 * nb // 4, nb, inner_rows, 0)
    for copy in e_copies:
        copy.wait()
    wide_e[...] = sums_e[...].astype(F32)
    for k in range(nb):
        lanes = slice(k * LANES, (k + 1) * LANES)
        gr_out_ref[:, lanes] = wide_e[pl.ds(k // SUB * poles * SUB + k % SUB, poles, stride=SUB), :]
        gskip_out_ref[:, lanes] = wide_e[lines + k : lines + k + 1, :]
        conv_ref[0, :, lanes] = wide_e[pl.ds(first + k, TAPS, stride=nb), :]
    halo.wait()
    lax.fori_loop(0, nb, last_rows, 0)
    for copy in l_copies:
        copy.wait()
    wide_l[...] = sums_l[...].astype(F32)
    for k in range(nb):
        lanes = slice(k * LANES, (k + 1) * LANES)
        for f in range(1, 3):
            conv_ref[f, :, lanes] = wide_l[pl.ds((f - 1) * TAPS * nb + k, TAPS, stride=nb), :]


def finish_kernel(hyena_in, gn_in, conv_in, gr_in, gskip_in, hyena_ref, gn_ref, conv_ref, gr_ref, gskip_ref, sem):
    pairs = (
        (hyena_in, hyena_ref), (gn_in, gn_ref), (conv_in, conv_ref), (gr_in, gr_ref), (gskip_in, gskip_ref),
    )
    copies = [pltpu.make_async_copy(src, dst, sem.at[i]) for i, (src, dst) in enumerate(pairs)]
    for copy in copies:
        copy.start()
    for copy in copies:
        copy.wait()


def solution(mesh):
    n_seq, n_ch = mesh.shape["seq"], mesh.shape["ch"]
    dma = pltpu.SemaphoreType.DMA
    vmem = pltpu.VMEM

    def per_device(token_ids, embedding, norm_gain, conv_weight, pole_rates, residues, skip_gain, cotangent):
        length, chans = cotangent.shape
        poles = pole_rates.shape[0]
        nb = chans // LANES
        lines = poles * nb
        rp = poles * SUB // min(n_seq, poles)

        def reduced(rows):
            each = -(-rows // (16 * n_seq)) * 16
            return [
                vmem((each * n_seq, LANES), F32), vmem((each * n_seq, LANES), BF16), vmem((n_seq, each, LANES), BF16),
                vmem((each, LANES), BF16), vmem((each * n_seq, LANES), BF16), vmem((each * n_seq, LANES), F32),
            ]

        tile = vmem((length * (nb + GAP), LANES), F32)
        line = vmem((lines, LANES), F32)
        kept = vmem((length // CHUNK * lines, LANES), F32)
        scratch = [
            vmem((1, length), jnp.int32), vmem((1, chans), F32), vmem((3, TAPS, chans), F32),
            vmem((poles, chans), F32), vmem((poles, chans), F32), vmem((1, chans), F32), vmem((length, chans), BF16),
            dma((7,)),
            vmem((SUB, LANES), F32), vmem((n_ch, SUB, LANES), F32), vmem((1, length), jnp.int32),
            vmem((3, length, chans), BF16), tile, tile, vmem((4 * SUB, length), BF16), vmem((SUB, chans), F32),
            vmem((2, lines, LANES), F32), vmem((2, lines, LANES), F32), line, vmem((nb, LANES), F32),
            line, line, line, vmem((CHUNK * nb, LANES), F32), line, kept, kept, line, tile, tile, vmem((3, 8 * SUB, chans), BF16),
            vmem((2, nb // SUB, n_seq, rp, LANES), F32), vmem((2, nb // SUB, n_seq, rp, LANES), F32),
            vmem((3, length, chans), BF16), vmem((3, SUB, chans), BF16), vmem((3, SUB, chans), BF16),
            *reduced(lines + nb + TAPS * nb), *reduced(2 * TAPS * nb), vmem((3, length + SUB, LANES), F32),
            vmem((BAND, chans), BF16), dma, dma((n_ch,)), dma((n_ch,)), dma((4,)),
        ] + [dma((2, nb // SUB, n_seq))] * 4 + [dma((n_seq,))] * 8
        outs = [
            ((length, chans), BF16), ((length, chans), BF16), ((3, TAPS, chans), F32), ((poles, chans), F32),
            ((1, chans), F32),
        ]
        ins = (
            token_ids.reshape(1, length), embedding, norm_gain.reshape(1, chans), conv_weight, pole_rates, residues,
            skip_gain.reshape(1, chans), cotangent,
        )
        held = pl.pallas_call(
            functools.partial(mega_kernel, n_seq, n_ch, poles),
            out_shape=[pltpu.VMEM(shape, dtype) for shape, dtype in outs],
            in_specs=[
                pl.BlockSpec(memory_space=pl.ANY) for i in range(len(ins))
            ],
            out_specs=[pl.BlockSpec(memory_space=pltpu.VMEM)] * len(outs),
            scratch_shapes=scratch,
            compiler_params=pltpu.CompilerParams(
                vmem_limit_bytes=VLIMIT, collective_id=0, has_side_effects=True
            ),
        )(*ins)
        hyena, grad_normed, conv, gr, gskip = pl.pallas_call(
            finish_kernel,
            out_shape=[jax.ShapeDtypeStruct(shape, dtype) for shape, dtype in outs],
            in_specs=[pl.BlockSpec(memory_space=pltpu.VMEM)] * len(outs),
            out_specs=[pl.BlockSpec(memory_space=pl.ANY)] * len(outs),
            scratch_shapes=[dma((len(outs),))],
        )(*(pltpu.with_memory_space_constraint(part, pltpu.VMEM) for part in held))
        return hyena, grad_normed, conv, gr, gskip.reshape(chans)

    in_specs = (
        P("seq"), P(None, "ch"), P("ch"), P(None, None, "ch"), P(None, "ch"), P(None, "ch"), P("ch"), P("seq", "ch"),
    )
    out_specs = (P("seq", "ch"), P("seq", "ch"), P(None, None, "ch"), P(None, "ch"), P("ch"))
    return jax.shard_map(per_device, mesh=mesh, in_specs=in_specs, out_specs=out_specs, check_vma=False)
```

```python
import functools

import jax
import jax.numpy as jnp
from jax import lax
from jax.experimental import pallas as pl
from jax.experimental.pallas import tpu as pltpu
from jax.sharding import PartitionSpec as P

TAPS = 7
CODES = (65, 67, 71, 84)
MESH = pl.DeviceIdType.MESH
F32 = jnp.float32
BF16 = jnp.bfloat16
LANES = 128
SUB = 8
CHUNK = 8
GAP = 8
PAIR = 2
BAND = 32
VLIMIT = 60 * 1024 * 1024


def greet(peers):
    barrier = pltpu.get_barrier_semaphore()
    for peer in peers:
        pl.semaphore_signal(barrier, inc=1, device_id=peer, device_id_type=MESH)


def greeted(peers):
    pl.semaphore_wait(pltpu.get_barrier_semaphore(), len(peers))


def remote(src, dst, send_sem, recv_sem, peer):
    return pltpu.make_async_remote_copy(
        src_ref=src, dst_ref=dst, send_sem=send_sem, recv_sem=recv_sem,
        device_id=peer, device_id_type=MESH,
    )


def mega_kernel(
    n_seq, n_ch, poles,
    ids_in, emb_ref, gain_in, w_in, rate_in, res_in, skip_in, ct_in,
    hyena_ref, gn_ref, conv_ref, gr_out_ref, gskip_out_ref,
    ids_ref, gain_ref, w_ref, rate_ref, res_ref, skip_in_ref, ct_ref, load_sem,
    part, ss_got, prev_got, feat_ref, y_ref, gm_ref, ot_ref, n4_ref, ends_ref, in_ref, gr_ref, gskip_ref,
    p_ref, rp_ref, pc_ref, hs_ref, lag_ref, s0_ref, b0_ref, decay_ref, xs, gs, table, got, out, fg_ref, head_ref, tail,
    terms_e, whole_e, tgot_e, total_e, sums_e, wide_e, terms_l, whole_l, tgot_l, total_l, sums_l, wide_l, pad,
    emb_rows, emb_sem, ss_send, ss_recv, halo_sem, x_send, x_recv, xb_send, xb_recv,
    t_send, t_recv, tb_send, tb_recv, l_send, l_recv, lb_send, lb_recv,
):
    me = lax.axis_index("seq")
    ch = lax.axis_index("ch")
    length, chans = ct_ref.shape
    width = chans * n_ch
    nb = chans // LANES
    pitch = nb + GAP
    lines = poles * nb
    first = lines + nb
    peer = [lax.rem(me + o, n_seq) for o in range(n_seq)]
    ch_peer = [lax.rem(ch + o, n_ch) for o in range(n_ch)]

    peers = [{"seq": peer[o]} for o in range(1, n_seq)] + [{"ch": ch_peer[o]} for o in range(1, n_ch)]
    greet(peers)
    low_row = min(CODES) // BAND * BAND
    fetch = pltpu.make_async_copy(emb_ref.at[low_row : low_row + BAND, :], emb_rows, emb_sem)
    fetch.start()
    loads = [
        pltpu.make_async_copy(src, dst, load_sem.at[i])
        for i, (src, dst) in enumerate((
            (rate_in, rate_ref), (res_in, res_ref), (skip_in, skip_in_ref), (ids_in, ids_ref), (gain_in, gain_ref),
            (w_in, w_ref), (ct_in, ct_ref),
        ))
    ]
    for load in loads:
        load.start()
    for load in loads[:3]:
        load.wait()
    for k in range(nb):
        lanes = slice(k * LANES, (k + 1) * LANES)
        rates = rate_ref[:, lanes]
        rows = pl.ds(k // SUB * poles * SUB + k % SUB, poles, stride=SUB)
        p_ref[rows, :] = jnp.exp(-rates)
        decay_ref[rows, :] = jnp.exp(-rates * length)
        pc_ref[rows, :] = jnp.exp(-rates * CHUNK)
        rp_ref[rows, :] = res_ref[:, lanes] * jnp.exp(-rates)
        weight = res_ref[:, lanes]
        for d in range(CHUNK):
            tap = jnp.sum(weight, axis=0, keepdims=True)
            hs_ref[d * nb + k : d * nb + k + 1, :] = tap + skip_in_ref[:, lanes] if d == 0 else tap
            weight = weight * jnp.exp(-rates)
    fetch.wait()
    emb = jnp.concatenate(
        [emb_rows[v - low_row : v - low_row + 1, :].astype(F32) for v in CODES] * 2,
        0,
    )
    squares = jnp.broadcast_to(jnp.sum(emb * emb, axis=1, keepdims=True), (SUB, LANES))
    part[...] = squares
    greeted(peers)
    ids_copy = remote(ids_in, prev_got, halo_sem.at[0], halo_sem.at[1], {"seq": peer[1]})
    ids_copy.start()
    copies = []
    for o in range(1, n_ch):
        copy = remote(part, ss_got.at[o], ss_send.at[o], ss_recv.at[o], {"ch": ch_peer[o]})
        copy.start()
        copies.append(copy)
    for load in loads[3:6]:
        load.wait()
    ids_copy.wait()
    prev = jnp.where(me > 0, prev_got[...], -1)
    row = lax.broadcasted_iota(jnp.int32, (SUB, length), 0)
    code = jnp.full((SUB, length), -2, jnp.int32)
    for a, value in enumerate(CODES):
        code = jnp.where(lax.rem(row, len(CODES)) == a, value, code)
    ext = jnp.concatenate([prev, ids_ref[...]], 1)
    shifted = [ext[:, length - i : 2 * length - i] for i in range(TAPS)] + [jnp.full((1, length), -1, jnp.int32)]
    hits = [
        jnp.where(jnp.where(row >= len(CODES), shifted[2 * j + 1], shifted[2 * j]) == code, 1.0, 0.0).astype(F32)
        for j in range(SUB // 2)
    ]
    onehot = jnp.concatenate(hits, 0)
    ot_ref[...] = onehot.astype(BF16)
    picks = jnp.transpose(jnp.concatenate([onehot] * 2, 0)).astype(BF16)
    for o in range(1, n_ch):
        copies[o - 1].wait()
        squares = squares + ss_got[o]
    scale = lax.rsqrt(squares / width + 1e-05)[:, :1]
    n4 = (emb * scale * gain_ref[...]).astype(BF16).astype(F32)
    n4_ref[...] = n4
    later = lax.broadcasted_iota(jnp.int32, (SUB, chans), 0) >= len(CODES)
    for f in range(3):
        w = [w_ref[f, i : i + 1, :] for i in range(TAPS)] + [jnp.zeros((1, chans), F32)]
        full = jnp.concatenate([jnp.where(later, w[2 * j + 1], w[2 * j]) * n4 for j in range(SUB // 2)], 0)
        high = full.astype(BF16)
        rest = full - high.astype(F32)
        table[f, 0 : 4 * SUB, :] = high
        table[f, 4 * SUB : 8 * SUB, :] = rest.astype(BF16)

    def feature_block(kb):
        lanes = pl.ds(pl.multiple_of(kb * 256, 256), 256)
        parts = []
        for f in range(3):
            val = jnp.dot(picks, table[f, :, lanes], preferred_element_type=F32).astype(BF16)
            feat_ref[f, :, lanes] = val
            parts.append(val.astype(F32))
        x = parts[1] * parts[2]
        g = ct_ref[:, lanes].astype(F32) * parts[0]
        for s in range(2):
            xs[pl.ds(kb * 2 + s, length, stride=pitch), :] = x[:, s * LANES : (s + 1) * LANES]
            gs[pl.ds(kb * 2 + s, length, stride=pitch), :] = g[:, s * LANES : (s + 1) * LANES]

    def features(step, carry):
        for b in range(4):
            feature_block(step * 4 + b)
        return carry

    loads[6].wait()
    lax.fori_loop(0, chans // 1024, features, 0)


    own = min(n_seq, poles)
    held = poles * SUB
    rp = held // own
    base = me // own * own
    back = [base + lax.rem(me - base + o, own) for o in range(own)]

    def chunk(k, h):
        return pl.ds(pl.multiple_of(h * held + lax.rem(k, own) * rp, rp), rp)

    def send_ends(side, h):
        started = []
        for o in range(1, n_seq):
            copy = remote(
                ends_ref.at[side, chunk(peer[o], h), :], got.at[side, h, me],
                x_send.at[side, h, o], x_recv.at[side, h, o], {"seq": peer[o]},
            )
            copy.start()
            started.append(copy)
        got[side, h, me] = ends_ref[side, chunk(me, h), :]
        return started

    def send_carries(side, h, started):
        for copy in started:
            copy.wait()
        decay = decay_ref[chunk(me, h), :]
        state = jnp.zeros_like(decay)
        for e in reversed(range(n_seq)) if side else range(n_seq):
            out[side, h, e] = state
            state = decay * state + got[side, h, e]
        started = []
        for o in range(1, own):
            copy = remote(
                out.at[side, h, back[o]], in_ref.at[side, chunk(me, h), :],
                xb_send.at[side, h, o], xb_recv.at[side, h, o], {"seq": back[o]},
            )
            copy.start()
            started.append(copy)
        in_ref[side, chunk(me, h), :] = out[side, h, me]
        return started

    group = poles // 2
    zero = jnp.zeros((SUB, LANES), F32)
    halves = range(nb // SUB)
    chunks = length // CHUNK
    at = [[pl.ds((h * poles + n) * SUB, SUB) for n in range(poles)] for h in halves]

    def row(ref_row, h):
        return pl.ds(pl.multiple_of(ref_row * nb + h * SUB, SUB), SUB)

    def time(t, h):
        return pl.ds(pl.multiple_of(t * pitch + h * SUB, SUB), SUB)

    def tree(values):
        values = list(values)
        while len(values) > 1:
            values = [
                values[i] + values[i + 1] if i + 1 < len(values) else values[i] for i in range(0, len(values), 2)
            ]
        return values[0]

    f_copies = []
    for h in halves:
        for half in range(2):
            poles_of = range(half * group, (half + 1) * group)
            p = [p_ref[at[h][n], :] for n in poles_of]
            pc = [pc_ref[at[h][n], :] for n in poles_of]

            def states(step, s):
                s = list(s)
                for c in range(PAIR):
                    u = step * PAIR + c
                    for i, n in enumerate(poles_of):
                        s0_ref[row(u * poles + n, h), :] = s[i]
                    for v in range(CHUNK):
                        x = xs[time(u * CHUNK + v, h), :]
                        e = [p[i] * e[i] + x for i in range(group)] if v else [x] * group
                    s = [pc[i] * s[i] + e[i] for i in range(group)]
                return tuple(s)

            s = lax.fori_loop(0, chunks // PAIR, states, (zero,) * group)
            for i, n in enumerate(poles_of):
                ends_ref[0, at[h][n], :] = s[i]
        f_copies.append(send_ends(0, h))

    a_copies = []
    for h in halves:
        for half in range(2):
            poles_of = range(half * group, (half + 1) * group)
            p = [p_ref[at[h][n], :] for n in poles_of]
            pc = [pc_ref[at[h][n], :] for n in poles_of]

            def adjoints(step, carry):
                s, acc = list(carry[0]), list(carry[1])
                for c in range(PAIR):
                    u = chunks - 1 - (step * PAIR + c)
                    for i, n in enumerate(poles_of):
                        b0_ref[row(u * poles + n, h), :] = s[i]
                    for v in reversed(range(CHUNK)):
                        g = gs[time(u * CHUNK + v, h), :]
                        e = [p[i] * e[i] + g for i in range(group)] if v < CHUNK - 1 else [g] * group
                    s = [pc[i] * s[i] + e[i] for i in range(group)]
                    acc = [acc[i] + s0_ref[row(u * poles + n, h), :] * e[i] for i, n in enumerate(poles_of)]
                return tuple(s), tuple(acc)

            s, acc = lax.fori_loop(0, chunks // PAIR, adjoints, ((zero,) * group, (zero,) * group))
            for i, n in enumerate(poles_of):
                ends_ref[1, at[h][n], :] = s[i]
                gr_ref[at[h][n], :] = acc[i]
        f_copies[h] = send_carries(0, h, f_copies[h])
        a_copies.append(send_ends(1, h))

    for h in halves:
        taps = [hs_ref[row(d, h), :] for d in range(CHUNK)]

        def near_chunk(u, lag):
            lag = list(lag)
            x = [xs[time(u * CHUNK + v, h), :] for v in range(CHUNK)]
            g = [gs[time(u * CHUNK + v, h), :] for v in range(CHUNK)]
            for v in range(CHUNK):
                y_ref[time(u * CHUNK + v, h), :] = tree(taps[d] * x[v - d] for d in range(v + 1))
                gm_ref[time(u * CHUNK + v, h), :] = tree(taps[d] * g[v + d] for d in range(CHUNK - v))
            for d in range(CHUNK):
                lag[d] = lag[d] + tree(g[v + d] * x[v] for v in range(CHUNK - d))
            return tuple(lag)

        def near(step, lag):
            for c in range(PAIR):
                lag = near_chunk(step * PAIR + c, lag)
            return lag

        lag = lax.fori_loop(0, chunks // PAIR, near, (zero,) * CHUNK)
        gskip_ref[h * SUB : (h + 1) * SUB, :] = lag[0]
        for n in range(poles):
            p = p_ref[at[h][n], :]
            total_lag = lag[CHUNK - 1]
            for d in reversed(range(CHUNK - 1)):
                total_lag = p * total_lag + lag[d]
            lag_ref[at[h][n], :] = total_lag

    def far(side, h, started, kept, ref):
        for copy in started:
            copy.wait()
        p = [p_ref[at[h][n], :] for n in range(poles)]

        def readout_chunk(step, w):
            u = chunks - 1 - step if side else step
            part = [rp_ref[at[h][n], :] * kept[row(u * poles + n, h), :] + w[n] for n in range(poles)]
            for v in reversed(range(CHUNK)) if side else range(CHUNK):
                rows = time(u * CHUNK + v, h)
                ref[rows, :] = ref[rows, :] + tree(part)
                part = [part[n] * p[n] for n in range(poles)]
            return tuple(w[n] * pc_ref[at[h][n], :] for n in range(poles))

        def readout(step, w):
            for c in range(PAIR):
                w = readout_chunk(step * PAIR + c, w)
            return w

        lax.fori_loop(0, chunks // PAIR, readout, tuple(rp_ref[a, :] * in_ref[side, a, :] for a in at[h]))

    for h in halves:
        a_copies[h] = send_carries(1, h, a_copies[h])
        far(0, h, f_copies[h], s0_ref, y_ref)
    terms_e[0:lines, :] = p_ref[...] * (gr_ref[...] + in_ref[0] * ends_ref[1]) + lag_ref[...]
    terms_e[lines:first, :] = gskip_ref[...]
    for ref, used in ((terms_e, first + TAPS * nb), (terms_l, 2 * TAPS * nb)):
        if used < ref.shape[0]:
            ref[used:, :] = jnp.zeros((ref.shape[0] - used, LANES), F32)
    hits_t = ot_ref[...]
    wide_lanes = 2 * LANES

    def emit(f, k, lanes, val, ref, base):
        val = val.astype(BF16)
        fg_ref[f, :, lanes] = val
        head_ref[f, :, lanes] = val[:SUB, :]
        sums = jnp.dot(hits_t, val, preferred_element_type=F32)
        n4 = n4_ref[:, lanes]
        taps = []
        for i in range(SUB // 2):
            pair = sums[i * SUB : (i + 1) * SUB, :] * n4
            pair = pair + pltpu.roll(pair, 2, 0)
            pair = pair + pltpu.roll(pair, 1, 0)
            taps += [pair[len(CODES) - 1 : len(CODES), :], pair[SUB - 1 : SUB, :]]
        taps = jnp.concatenate(taps[:TAPS], 0)
        for s in range(2):
            ref[pl.ds(base + k * 2 + s, TAPS, stride=nb), :] = taps[:, s * LANES : (s + 1) * LANES]

    def along(ref, k):
        return jnp.concatenate([ref[pl.ds(k * 2 + s, length, stride=pitch), :] for s in range(2)], 1)

    def query_outputs_block(k):
        lanes = pl.ds(pl.multiple_of(k * wide_lanes, wide_lanes), wide_lanes)
        y = along(y_ref, k)
        emit(0, k, lanes, ct_ref[:, lanes].astype(F32) * y, terms_e, first)

    def query_outputs(step, carry):
        for b in range(4):
            query_outputs_block(step * 4 + b)
        return carry

    def scatter(whole, ref, got_ref, send, recv):
        whole[...] = ref[...].astype(BF16)
        rows = whole.shape[0] // n_seq
        started = []
        for o in range(1, n_seq):
            mine = pl.ds(pl.multiple_of(peer[o] * rows, rows), rows)
            copy = remote(whole.at[mine, :], got_ref.at[o], send.at[o], recv.at[o], {"seq": peer[o]})
            copy.start()
            started.append(copy)
        return started

    def gather(started, whole, got_ref, total, sums, send, recv):
        rows = whole.shape[0] // n_seq
        mine = pl.ds(pl.multiple_of(me * rows, rows), rows)
        summed = whole[mine, :].astype(F32)
        for o in range(1, n_seq):
            started[o - 1].wait()
            summed = summed + got_ref[o].astype(F32)
        total[...] = summed.astype(BF16)
        started = []
        for o in range(1, n_seq):
            copy = remote(total, sums.at[mine, :], send.at[o], recv.at[o], {"seq": peer[o]})
            copy.start()
            started.append(copy)
        sums[mine, :] = summed.astype(BF16)
        return started

    lax.fori_loop(0, nb // 8, query_outputs, 0)
    e_copies = scatter(whole_e, terms_e, tgot_e, t_send, t_recv)
    for h in halves:
        far(1, h, a_copies[h], b0_ref, gm_ref)
        if h == 0:
            e_copies = gather(e_copies, whole_e, tgot_e, total_e, sums_e, tb_send, tb_recv)

    def key_outputs_block(k):
        lanes = pl.ds(pl.multiple_of(k * wide_lanes, wide_lanes), wide_lanes)
        gm = along(gm_ref, k)
        emit(1, k, lanes, gm * feat_ref[2, :, lanes].astype(F32), terms_l, 0)
        emit(2, k, lanes, gm * feat_ref[1, :, lanes].astype(F32), terms_l, TAPS * nb)

    def key_outputs(step, carry):
        for b in range(4):
            key_outputs_block(step * 4 + b)
        return carry

    lax.fori_loop(0, nb // 8, key_outputs, 0)
    l_copies = scatter(whole_l, terms_l, tgot_l, l_send, l_recv)
    halo = remote(head_ref, tail, halo_sem.at[2], halo_sem.at[3], {"seq": peer[n_seq - 1]})
    halo.start()
    keep = jnp.where(me < n_seq - 1, 1.0, 0.0).astype(F32)
    block = 64
    inner = length - block

    def filtered(k, begin, end, base):
        lanes = pl.ds(pl.multiple_of(k * LANES, LANES), LANES)
        w = [w_ref[f, i : i + 1, lanes] for f in range(3) for i in range(TAPS)]
        for b in range(begin, end, block):
            acc = jnp.zeros((block, LANES), F32)
            for f in range(3):
                for i in range(TAPS):
                    acc = acc + w[f * TAPS + i] * pad[f, b - base + i : b - base + i + block, :]
            gn_ref[b : b + block, lanes] = acc.astype(BF16)

    def inner_rows(k, carry):
        lanes = pl.ds(pl.multiple_of(k * LANES, LANES), LANES)
        for f in range(3):
            pad[f, 0:length, :] = fg_ref[f, :, lanes].astype(F32)
        filtered(k, 0, inner, 0)
        return carry

    def last_rows(k, carry):
        lanes = pl.ds(pl.multiple_of(k * LANES, LANES), LANES)
        for f in range(3):
            pad[f, 0:block, :] = fg_ref[f, inner:length, lanes].astype(F32)
            pad[f, block : block + SUB, :] = tail[f, :, lanes].astype(F32) * keep
        filtered(k, inner, length, inner)
        return carry

    def hyena_rows(k, carry):
        lanes = pl.ds(pl.multiple_of(k * wide_lanes, wide_lanes), wide_lanes)
        hyena_ref[:, lanes] = (feat_ref[0, :, lanes].astype(F32) * along(y_ref, k)).astype(BF16)
        return carry

    lax.fori_loop(0, nb // 2, hyena_rows, 0)
    lax.fori_loop(0, 3 * nb // 4, inner_rows, 0)
    l_copies = gather(l_copies, whole_l, tgot_l, total_l, sums_l, lb_send, lb_recv)
    lax.fori_loop(3 * nb // 4, nb, inner_rows, 0)
    for copy in e_copies:
        copy.wait()
    wide_e[...] = sums_e[...].astype(F32)
    for k in range(nb):
        lanes = slice(k * LANES, (k + 1) * LANES)
        gr_out_ref[:, lanes] = wide_e[pl.ds(k // SUB * poles * SUB + k % SUB, poles, stride=SUB), :]
        gskip_out_ref[:, lanes] = wide_e[lines + k : lines + k + 1, :]
        conv_ref[0, :, lanes] = wide_e[pl.ds(first + k, TAPS, stride=nb), :]
    halo.wait()
    lax.fori_loop(0, nb, last_rows, 0)
    for copy in l_copies:
        copy.wait()
    wide_l[...] = sums_l[...].astype(F32)
    for k in range(nb):
        lanes = slice(k * LANES, (k + 1) * LANES)
        for f in range(1, 3):
            conv_ref[f, :, lanes] = wide_l[pl.ds((f - 1) * TAPS * nb + k, TAPS, stride=nb), :]


def finish_kernel(hyena_in, gn_in, conv_in, gr_in, gskip_in, hyena_ref, gn_ref, conv_ref, gr_ref, gskip_ref, sem):
    pairs = (
        (hyena_in, hyena_ref), (gn_in, gn_ref), (conv_in, conv_ref), (gr_in, gr_ref), (gskip_in, gskip_ref),
    )
    copies = [pltpu.make_async_copy(src, dst, sem.at[i]) for i, (src, dst) in enumerate(pairs)]
    for copy in copies:
        copy.start()
    for copy in copies:
        copy.wait()


def solution(mesh):
    n_seq, n_ch = mesh.shape["seq"], mesh.shape["ch"]
    dma = pltpu.SemaphoreType.DMA
    vmem = pltpu.VMEM

    def per_device(token_ids, embedding, norm_gain, conv_weight, pole_rates, residues, skip_gain, cotangent):
        length, chans = cotangent.shape
        poles = pole_rates.shape[0]
        nb = chans // LANES
        lines = poles * nb
        rp = poles * SUB // min(n_seq, poles)

        def reduced(rows):
            each = -(-rows // (16 * n_seq)) * 16
            return [
                vmem((each * n_seq, LANES), F32), vmem((each * n_seq, LANES), BF16), vmem((n_seq, each, LANES), BF16),
                vmem((each, LANES), BF16), vmem((each * n_seq, LANES), BF16), vmem((each * n_seq, LANES), F32),
            ]

        tile = vmem((length * (nb + GAP), LANES), F32)
        line = vmem((lines, LANES), F32)
        kept = vmem((length // CHUNK * lines, LANES), F32)
        scratch = [
            vmem((1, length), jnp.int32), vmem((1, chans), F32), vmem((3, TAPS, chans), F32),
            vmem((poles, chans), F32), vmem((poles, chans), F32), vmem((1, chans), F32), vmem((length, chans), BF16),
            dma((7,)),
            vmem((SUB, LANES), F32), vmem((n_ch, SUB, LANES), F32), vmem((1, length), jnp.int32),
            vmem((3, length, chans), BF16), tile, tile, vmem((4 * SUB, length), BF16), vmem((SUB, chans), F32),
            vmem((2, lines, LANES), F32), vmem((2, lines, LANES), F32), line, vmem((nb, LANES), F32),
            line, line, line, vmem((CHUNK * nb, LANES), F32), line, kept, kept, line, tile, tile, vmem((3, 8 * SUB, chans), BF16),
            vmem((2, nb // SUB, n_seq, rp, LANES), F32), vmem((2, nb // SUB, n_seq, rp, LANES), F32),
            vmem((3, length, chans), BF16), vmem((3, SUB, chans), BF16), vmem((3, SUB, chans), BF16),
            *reduced(lines + nb + TAPS * nb), *reduced(2 * TAPS * nb), vmem((3, length + SUB, LANES), F32),
            vmem((BAND, chans), BF16), dma, dma((n_ch,)), dma((n_ch,)), dma((4,)),
        ] + [dma((2, nb // SUB, n_seq))] * 4 + [dma((n_seq,))] * 8
        outs = [
            ((length, chans), BF16), ((length, chans), BF16), ((3, TAPS, chans), F32), ((poles, chans), F32),
            ((1, chans), F32),
        ]
        ins = (
            token_ids.reshape(1, length), embedding, norm_gain.reshape(1, chans), conv_weight, pole_rates, residues,
            skip_gain.reshape(1, chans), cotangent,
        )
        held = pl.pallas_call(
            functools.partial(mega_kernel, n_seq, n_ch, poles),
            out_shape=[pltpu.VMEM(shape, dtype) for shape, dtype in outs],
            in_specs=[
                pl.BlockSpec(memory_space=pl.ANY) for i in range(len(ins))
            ],
            out_specs=[pl.BlockSpec(memory_space=pltpu.VMEM)] * len(outs),
            scratch_shapes=scratch,
            compiler_params=pltpu.CompilerParams(
                vmem_limit_bytes=VLIMIT, collective_id=0, has_side_effects=True
            ),
        )(*ins)
        hyena, grad_normed, conv, gr, gskip = pl.pallas_call(
            finish_kernel,
            out_shape=[jax.ShapeDtypeStruct(shape, dtype) for shape, dtype in outs],
            in_specs=[pl.BlockSpec(memory_space=pltpu.VMEM)] * len(outs),
            out_specs=[pl.BlockSpec(memory_space=pl.ANY)] * len(outs),
            scratch_shapes=[dma((len(outs),))],
        )(*(pltpu.with_memory_space_constraint(part, pltpu.VMEM) for part in held))
        return hyena, grad_normed, conv, gr, gskip.reshape(chans)

    in_specs = (
        P("seq"), P(None, "ch"), P("ch"), P(None, None, "ch"), P(None, "ch"), P(None, "ch"), P("ch"), P("seq", "ch"),
    )
    out_specs = (P("seq", "ch"), P("seq", "ch"), P(None, None, "ch"), P(None, "ch"), P("ch"))
    return jax.shard_map(per_device, mesh=mesh, in_specs=in_specs, out_specs=out_specs, check_vma=False)
```
